32 devices in a mesh: grp: 2 (over x), seq: 4 (over y, core), tp: 4 (over z).
Axes of the slice: x: 2, y: 2, z: 4, core: 2. Of those that a mesh axis runs over, the one named last changes fastest.
Arguments:
- prompt: bfloat16 [2048, 5376], P(('grp', 'seq'), 'tp'), parts along dimension 0, may hold values from -8 to 8, as said below
- cont_ids: int32 [16, 64], P('grp'), parts along dimension 0, may hold values from 0 to 131071
- embed: bfloat16 [131072, 5376], P('seq', 'tp'), may hold values from -0.078125 to 0.078125
- pre_gain: float32 [5376], replicated, may hold values from 0.5 to 1.5
- w_query: bfloat16 [5376, 4096], P('seq', 'tp'), may hold values from -0.078125 to 0.078125
- w_keyval: bfloat16 [5376, 2, 2048], P('seq', None, 'tp'), may hold values from -0.078125 to 0.078125
- q_gain: float32 [128], replicated, may hold values from 0.25 to 1.75
- k_gain: float32 [128], replicated, may hold values from 0.25 to 1.75
- w_out: bfloat16 [4096, 5376], P('tp', 'seq'), may hold values from -0.09375 to 0.09375
- post_gain: float32 [5376], replicated, may hold values from 0.5 to 1.5
Outputs:
- prompt_out: bfloat16 [2048, 5376], P(('grp', 'seq'), 'tp'), parts along dimension 0
- cont_out: bfloat16 [16, 64, 5376], P(('grp', 'seq'), None, 'tp'), parts along dimension 0
The draws below stay inside these ranges and needn't reach their ends.
There are 2 independent parts, one for each index of `grp`. The reference program is written for one: setup_inputs(seed, part) draws one part's arguments, and reference() takes and returns one part's arrays. A program takes and returns all parts, laid end to end along the dimension named above; an argument that names none is the same for every part. Nothing has to cross between parts.
Inputs may be any that keep to these rules, and one draw needn't show every extreme that they name: `prompt`: values are rough from entry to entry.
All inputs are finite; a program needn't handle non-finite values.
Results may differ from the reference program's by a relative error of at most 0.014.
Values may be sent and summed in bfloat16 or wider, within the bound.
No kernel may reach another device: no remote copies, remote signals or barrier semaphores. Data moves between devices by JAX's collectives and lax.ppermute only.
A program may use at most 256 MiB of HBM per device.

```python
import math
import jax
import jax.numpy as jnp
import numpy as np
from jax import lax

D = 5376
HEADS = 32
KV = 16
HD = 128
WINDOW = 1024
VOCAB = 131072
TOK_DEV = 256
CLEN = 64
TOKENS = 1024
CONTS = 8
N_SEQ = 4
N_TP = 4


def draw_prompt(key, part):
    k_base, k_cols = jax.random.split(key, 2)
    cols = jnp.arange(D, dtype=jnp.float32) / D
    col_scale = 3.0 ** cols * jnp.exp(jax.random.uniform(k_cols, (D,), jnp.float32, -1.15, 1.15))
    base = jax.random.normal(k_base, (TOKENS, D), jnp.float32)
    values = base * col_scale / 1.5
    return jnp.clip(values, -8.0, 8.0).astype(jnp.bfloat16)


def with_ends(values, stream_key, smallest, high):
    longest = values.shape.index(max(values.shape))
    spots = []
    for shift in (0, 1):
        where = [jax.random.randint(jax.random.fold_in(stream_key, axis), (), 0, length) for axis, length in enumerate(values.shape)]
        where[longest] = (where[longest] + shift) % values.shape[longest]
        spots.append(tuple(where))
    return values.at[spots[0]].set(smallest).at[spots[1]].set(high)


def block_scale(rng, dims, cuts, low, high):
    level = 1.0
    for dim, parts in cuts:
        heights = jax.random.uniform(jax.random.fold_in(jax.random.fold_in(rng, 6), dim), (parts,), jnp.float32, low / len(cuts), high / len(cuts))
        level = level * jnp.repeat(jnp.exp(heights), dims[dim] // parts).reshape((-1,) + (1,) * (len(dims) - 1 - dim))
    return level


def skewed_wide(key, extent, count, lean):
    loads = [min(1 << octave, count + 1 - (1 << octave)) * (1 << 20) // math.isqrt((1 << octave) ** lean) + 1 for octave in range((count + 1).bit_length()) if 1 << octave <= count]
    spread = 1 + sum(loads) // (1 << 30)
    grid = np.cumsum(np.array([max(1, weight // spread) for weight in loads]))
    lot = jax.random.randint(jax.random.fold_in(key, 1), extent, 0, int(grid[len(loads) - 1]))
    start = jnp.left_shift(1, jnp.searchsorted(jnp.asarray(grid, jnp.int32), lot, side="right").astype(jnp.int32))
    grade = start - 1 + jax.random.randint(jax.random.fold_in(key, 4), extent, 0, 1 << 30) % jnp.minimum(start, count + 1 - start)
    return jax.random.permutation(jax.random.fold_in(key, 2), count)[grade].astype(jnp.int32)


def gaussian(own_key, dims, scale, reach, cuts=(), held_as=jnp.bfloat16):
    values = scale * jax.random.normal(own_key, dims, jnp.float32)
    if cuts:
        values = values * block_scale(own_key, dims, cuts, -0.22, 0.18)
    return jnp.clip(values, -reach, reach).astype(held_as)


def setup_inputs(seed: int = 0, part: int = 0) -> dict:
    seeds = jax.random.split(jax.random.key(seed), 11)
    part_splits = jax.random.split(jax.random.fold_in(seeds[10], part), 11)
    return {
        "prompt": draw_prompt(jax.random.fold_in(jax.random.fold_in(seeds[10], part), 71), part),
        "cont_ids": with_ends(skewed_wide(part_splits[1], (CONTS, CLEN), VOCAB, 2), jax.random.fold_in(part_splits[1], 3), 0, VOCAB - 1).astype(jnp.int32),
        "embed": gaussian(seeds[2], (VOCAB, D), D ** -0.5, 0.078125, ((0, 4), (1, 4))),
        "pre_gain": jnp.clip(1.0 + 0.1 * jax.random.normal(seeds[3], (D,), jnp.float32), 0.5, 1.5),
        "w_query": gaussian(seeds[4], (D, HEADS * HD), D ** -0.5, 0.078125, ((0, 4), (1, 4))),
        "w_keyval": gaussian(seeds[5], (D, 2, KV * HD), D ** -0.5, 0.078125, ((0, 4), (2, 4))),
        "q_gain": jnp.clip(1.0 + 0.15 * jax.random.normal(seeds[6], (HD,), jnp.float32), 0.25, 1.75),
        "k_gain": jnp.clip(1.0 + 0.15 * jax.random.normal(seeds[7], (HD,), jnp.float32), 0.25, 1.75),
        "w_out": gaussian(seeds[8], (HEADS * HD, D), (HEADS * HD) ** -0.5, 0.09375, ((0, 4), (1, 4))),
        "post_gain": jnp.clip(1.0 + 0.1 * jax.random.normal(seeds[9], (D,), jnp.float32), 0.5, 1.5),
    }


eps_norm = 1e-06
query_scalar = 168.0
rope_base = 10000.0

def rms_scale(values, gain):
    mean_sq = lax.optimization_barrier(jnp.mean(values * values, axis=-1, keepdims=True))
    return values * lax.rsqrt(mean_sq + eps_norm) * gain

def rotate(values, positions):
    half = values.shape[-1] // 2
    freqs = rope_base ** (-(jnp.arange(half, dtype=jnp.int32).astype(jnp.float32) * 2.0) / values.shape[-1])
    angles = positions.astype(jnp.float32)[:, None] * freqs[None, :]
    cosine = jnp.cos(angles)[:, None, :]
    sine = jnp.sin(angles)[:, None, :]
    first = values[..., :half]
    second = values[..., half:]
    return jnp.concatenate([first * cosine - second * sine, second * cosine + first * sine], axis=-1)

def attend(queries, keys, values, allowed):
    rows, heads, width = queries.shape
    kv_heads = keys.shape[1]
    grouped = queries.reshape(rows, kv_heads, heads // kv_heads, width).astype(jnp.float32)
    scores = jnp.einsum('qkgd,nkd->kgqn', grouped, keys.astype(jnp.float32)) * query_scalar ** (-0.5)
    scores = jnp.where(allowed[None, None], scores, -1e+30)
    top = lax.optimization_barrier(jnp.max(scores, axis=-1, keepdims=True))
    weights = jnp.exp(scores - top)
    weights = (weights / lax.optimization_barrier(jnp.sum(weights, axis=-1, keepdims=True))).astype(jnp.bfloat16)
    mixed = jnp.einsum('kgqn,nkd->qkgd', weights.astype(jnp.float32), values.astype(jnp.float32))
    return mixed.reshape(rows, heads * width).astype(jnp.bfloat16)

def reference(prompt, cont_ids, embed, pre_gain, w_query, w_keyval, q_gain, k_gain, w_out, post_gain):
    cont_rows = CONTS * CLEN
    picked = jnp.take(embed, cont_ids.reshape(-1), axis=0)
    cont_x = (picked.astype(jnp.float32) * math.sqrt(D)).astype(jnp.bfloat16)
    rows_x = jnp.concatenate([prompt, cont_x], axis=0)
    all_rows = rows_x.shape[0]
    normed = rms_scale(rows_x.astype(jnp.float32), pre_gain).astype(jnp.bfloat16)
    query_all = jnp.dot(normed, w_query, preferred_element_type=jnp.float32)
    keyval_all = jnp.einsum('rd,dcf->rcf', normed.astype(jnp.float32), w_keyval.astype(jnp.float32))
    positions = jnp.concatenate([jnp.arange(TOKENS, dtype=jnp.int32), TOKENS + jnp.arange(cont_rows, dtype=jnp.int32) % CLEN])
    queries = rotate(rms_scale(query_all.reshape(all_rows, HEADS, HD), q_gain), positions).astype(jnp.bfloat16)
    keys = rotate(rms_scale(keyval_all[:, 0].reshape(all_rows, KV, HD), k_gain), positions).astype(jnp.bfloat16)
    values = keyval_all[:, 1].reshape(all_rows, KV, HD).astype(jnp.bfloat16)
    pad_keys = jnp.concatenate([jnp.zeros((WINDOW, KV, HD), jnp.bfloat16), keys[:TOKENS]], axis=0)
    pad_values = jnp.concatenate([jnp.zeros((WINDOW, KV, HD), jnp.bfloat16), values[:TOKENS]], axis=0)

    def block(index):
        first = index * TOK_DEV
        q_blk = lax.dynamic_slice_in_dim(queries, first, TOK_DEV)
        k_blk = lax.dynamic_slice_in_dim(pad_keys, first, WINDOW + TOK_DEV)
        v_blk = lax.dynamic_slice_in_dim(pad_values, first, WINDOW + TOK_DEV)
        q_pos = first + jnp.arange(TOK_DEV, dtype=jnp.int32)
        key_pos = first - WINDOW + jnp.arange(WINDOW + TOK_DEV, dtype=jnp.int32)
        allowed = (key_pos[None, :] <= q_pos[:, None]) & (key_pos[None, :] > q_pos[:, None] - WINDOW) & (key_pos[None, :] >= 0)
        return attend(q_blk, k_blk, v_blk, allowed)
    prompt_mix = lax.map(block, jnp.arange(N_SEQ, dtype=jnp.int32)).reshape(TOKENS, HEADS * HD)
    final_keys = keys[TOKENS - WINDOW:TOKENS]
    final_values = values[TOKENS - WINDOW:TOKENS]
    spots = jnp.arange(CLEN, dtype=jnp.int32)
    allowed_cont = jnp.concatenate([jnp.arange(WINDOW, dtype=jnp.int32)[None, :] > spots[:, None], spots[None, :] <= spots[:, None]], axis=1)
    cont_q = queries[TOKENS:].reshape(CONTS, CLEN, HEADS, HD)
    cont_k = keys[TOKENS:].reshape(CONTS, CLEN, KV, HD)
    cont_v = values[TOKENS:].reshape(CONTS, CLEN, KV, HD)

    def one_cont(args):
        q_blk, k_blk, v_blk = args
        return attend(q_blk, jnp.concatenate([final_keys, k_blk], axis=0), jnp.concatenate([final_values, v_blk], axis=0), allowed_cont)
    cont_mix = lax.map(one_cont, (cont_q, cont_k, cont_v)).reshape(cont_rows, HEADS * HD)
    mixed = jnp.concatenate([prompt_mix, cont_mix], axis=0)
    per_group = HEADS * HD // N_TP
    attn_proj = jnp.zeros((all_rows, D), jnp.float32)
    for group in range(N_TP):
        part = jnp.dot(mixed[:, group * per_group:(group + 1) * per_group], w_out[group * per_group:(group + 1) * per_group], preferred_element_type=jnp.float32)
        rounded = lax.optimization_barrier(part.astype(jnp.bfloat16))
        attn_proj = attn_proj + rounded.astype(jnp.float32)
    result = (rows_x.astype(jnp.float32) + rms_scale(attn_proj, post_gain)).astype(jnp.bfloat16)
    return (result[:TOKENS], result[TOKENS:].reshape(CONTS, CLEN, D))
```

```python
import functools
import math

import jax
import jax.numpy as jnp
from jax import lax
from jax.experimental import pallas as pl
from jax.experimental.pallas import tpu as pltpu
from jax.sharding import PartitionSpec as P

WINDOW = 1024


eps_norm = 1e-06
query_scalar = 168.0
rope_base = 10000.0


def from_behind(value, axis, by):
    count = lax.axis_size(axis)
    pairs = [(i, i + by) for i in range(count) if 0 <= i + by < count]
    return lax.ppermute(value, axis, pairs)


def from_root(value, axis, root):
    mine = lax.axis_index(axis) == root
    return lax.psum(jnp.where(mine, value, jnp.zeros_like(value)), axis)


def rms_scale(values, gain):
    mean_sq = jnp.mean(values * values, axis=-1, keepdims=True)
    return values * lax.rsqrt(mean_sq + eps_norm) * gain


def rotate(values, positions):
    half = values.shape[-1] // 2
    freqs = rope_base ** (
        -(jnp.arange(half, dtype=jnp.int32).astype(jnp.float32) * 2.0) / values.shape[-1]
    )
    angles = positions.astype(jnp.float32)[:, None] * freqs[None, :]
    cosine = jnp.cos(angles)[:, None, :]
    sine = jnp.sin(angles)[:, None, :]
    first = values[..., :half]
    second = values[..., half:]
    return jnp.concatenate(
        [first * cosine - second * sine, second * cosine + first * sine], axis=-1
    )


def attend(queries, keys, values, allowed):
    rows, heads, width = queries.shape
    kv_heads = keys.shape[1]
    grouped = queries.reshape(rows, kv_heads, heads // kv_heads, width)
    scores = jnp.einsum(
        "qkgd,nkd->kgqn", grouped, keys, preferred_element_type=jnp.float32
    ) * query_scalar ** (-0.5)
    scores = jnp.where(allowed[None, None], scores, -1e30)
    top = jnp.max(scores, axis=-1, keepdims=True)
    weights = jnp.exp(scores - top)
    weights = (weights / jnp.sum(weights, axis=-1, keepdims=True)).astype(jnp.bfloat16)
    mixed = jnp.einsum("kgqn,nkd->qkgd", weights, values, preferred_element_type=jnp.float32)
    return mixed.reshape(rows, heads * width).astype(jnp.bfloat16)


def plain_device(
    prompt, cont_ids, embed, pre_gain, w_query, w_keyval, q_gain, k_gain, w_out, post_gain
):
    tok_rows, local_cols = prompt.shape
    n_seq = lax.axis_size("seq")
    n_tp = lax.axis_size("tp")
    seq_index = lax.axis_index("seq")
    tp_index = lax.axis_index("tp")
    full_width = local_cols * n_tp
    cont_count, cont_len = cont_ids.shape
    own_conts = cont_count // n_seq
    cont_rows = own_conts * cont_len
    vocab_rows = embed.shape[0]
    flat_ids = cont_ids.reshape(-1)
    vocab_start = seq_index * vocab_rows
    chosen = flat_ids - vocab_start
    inside = (chosen >= 0) & (chosen < vocab_rows)
    picked = jnp.take(embed, jnp.clip(chosen, 0, vocab_rows - 1), axis=0)
    embedded = lax.psum_scatter(
        jnp.where(inside[:, None], picked.astype(jnp.float32), 0.0).astype(jnp.bfloat16),
        "seq",
        scatter_dimension=0,
        tiled=True,
    ).astype(jnp.float32)
    cont_x = (embedded * math.sqrt(full_width)).astype(jnp.bfloat16)
    rows_x = jnp.concatenate([prompt, cont_x], axis=0)
    whole = lax.all_gather(rows_x, "tp", axis=1, tiled=True)
    normed = rms_scale(whole.astype(jnp.float32), pre_gain).astype(jnp.bfloat16)
    all_rows = normed.shape[0]
    q_cols = w_query.shape[1]
    kv_cols = w_keyval.shape[2]
    query_part = jnp.dot(
        normed,
        lax.all_gather(w_query, "seq", axis=0, tiled=True),
        preferred_element_type=jnp.float32,
    )
    kv_part = jnp.einsum(
        "rd,dcf->rcf",
        normed,
        lax.all_gather(w_keyval, "seq", axis=0, tiled=True),
        preferred_element_type=jnp.float32,
    )
    head_dim = q_gain.shape[0]
    q_heads = q_cols // head_dim
    kv_heads = kv_cols // head_dim
    tokens_total = n_seq * tok_rows
    positions = jnp.concatenate(
        [
            seq_index * tok_rows + jnp.arange(tok_rows, dtype=jnp.int32),
            tokens_total + jnp.arange(cont_rows, dtype=jnp.int32) % cont_len,
        ]
    )
    queries = rotate(
        rms_scale(query_part.reshape(all_rows, q_heads, head_dim), q_gain), positions
    ).astype(jnp.bfloat16)
    keys = rotate(
        rms_scale(kv_part[:, 0].reshape(all_rows, kv_heads, head_dim), k_gain), positions
    ).astype(jnp.bfloat16)
    values = kv_part[:, 1].astype(jnp.bfloat16)
    keyval = jnp.stack([keys.reshape(all_rows, kv_cols), values], axis=1)
    prompt_kv = keyval[:tok_rows]
    cont_kv = keyval[tok_rows:]
    reach = WINDOW // tok_rows
    earlier = []
    moving = prompt_kv
    for step in range(reach):
        moving = from_behind(moving, "seq", 1)
        earlier = [moving] + earlier
    band = jnp.concatenate(earlier + [prompt_kv], axis=0)
    q_pos = positions[:tok_rows]
    key_pos = seq_index * tok_rows - reach * tok_rows + jnp.arange(band.shape[0], dtype=jnp.int32)
    allowed = (
        (key_pos[None, :] <= q_pos[:, None])
        & (key_pos[None, :] > q_pos[:, None] - WINDOW)
        & (key_pos[None, :] >= 0)
    )
    prompt_mix = attend(
        queries[:tok_rows],
        band[:, 0].reshape(-1, kv_heads, head_dim),
        band[:, 1].reshape(-1, kv_heads, head_dim),
        allowed,
    )
    final = from_root(band[band.shape[0] - WINDOW :], "seq", n_seq - 1)
    spots = jnp.arange(cont_len, dtype=jnp.int32)
    allowed_cont = jnp.concatenate(
        [
            jnp.arange(WINDOW, dtype=jnp.int32)[None, :] > spots[:, None],
            spots[None, :] <= spots[:, None],
        ],
        axis=1,
    )
    cont_q = queries[tok_rows:].reshape(own_conts, cont_len, q_heads, head_dim)
    cont_keys = cont_kv.reshape(own_conts, cont_len, 2, kv_cols)

    def one_cont(query_block, key_block):
        joined = jnp.concatenate([final, key_block], axis=0)
        return attend(
            query_block,
            joined[:, 0].reshape(-1, kv_heads, head_dim),
            joined[:, 1].reshape(-1, kv_heads, head_dim),
            allowed_cont,
        )

    cont_mix = jax.vmap(one_cont)(cont_q, cont_keys).reshape(cont_rows, q_cols)
    mixed = jnp.concatenate([prompt_mix, cont_mix], axis=0)
    partial_rows = jnp.dot(
        mixed, lax.all_gather(w_out, "seq", axis=1, tiled=True), preferred_element_type=jnp.float32
    )
    attn_proj = lax.psum_scatter(
        partial_rows.astype(jnp.bfloat16), "tp", scatter_dimension=1, tiled=True
    ).astype(jnp.float32)
    row_sq = lax.psum(jnp.sum(attn_proj * attn_proj, axis=1), "tp")
    factor = lax.rsqrt(row_sq / full_width + eps_norm)
    gain_part = lax.dynamic_slice_in_dim(post_gain, tp_index * local_cols, local_cols)
    result = (rows_x.astype(jnp.float32) + attn_proj * factor[:, None] * gain_part).astype(
        jnp.bfloat16
    )
    return (result[:tok_rows], result[tok_rows:].reshape(own_conts, cont_len, local_cols))


ANY = pl.BlockSpec(memory_space=pl.ANY)
SMEM = pl.BlockSpec(memory_space=pltpu.SMEM)
VMEM = pl.BlockSpec(memory_space=pltpu.VMEM)
BATCH = 8


def pick_kernel(info, emb, tgt, out_a, out_b, buf, acc, sems):
    count = info[0]
    rounds = (count + BATCH - 1) // BATCH
    width = BATCH * 128

    def copies(step, slot):
        for b in range(BATCH):
            block = info[1 + step * BATCH + b]
            yield pltpu.make_async_copy(
                emb.at[:, pl.ds(pl.multiple_of(block * 128, 128), 128)],
                buf.at[slot, :, pl.ds(b * 128, 128)],
                sems.at[slot, b],
            )

    acc[...] = jnp.zeros_like(acc)

    @pl.when(rounds > 0)
    def _():
        for copy in copies(0, 0):
            copy.start()

    def body(step, carry):
        slot = lax.rem(step, 2)

        @pl.when(step + 1 < rounds)
        def _():
            for copy in copies(step + 1, 1 - slot):
                copy.start()

        for copy in copies(step, slot):
            copy.wait()
        rel = tgt[...] - step * width
        hot = lax.broadcasted_iota(jnp.int32, (width, rel.shape[1]), 0) == rel
        acc[...] += jnp.dot(
            buf[slot], hot.astype(jnp.bfloat16), preferred_element_type=jnp.float32
        )
        return carry

    lax.fori_loop(0, rounds, body, 0)
    half = out_a.shape[1]
    out_a[...] = acc[:, :half].astype(jnp.bfloat16)
    out_b[...] = acc[:, half:].astype(jnp.bfloat16)


def pick_rows(emb_t, flat_ids, vocab_start):
    width, vocab = emb_t.shape
    blocks = vocab // 128
    ids = flat_ids - vocab_start
    inside = (ids >= 0) & (ids < vocab)
    block = jnp.where(inside, ids >> 7, -1)
    number = jnp.arange(blocks, dtype=jnp.int32)
    equal = block[None, :] == number[:, None]
    present = jnp.any(equal, axis=1)
    rank = jnp.sum(
        jnp.where((number[None, :] < number[:, None]) & present[None, :], 1, 0), axis=1
    )
    listed = jnp.sum(
        jnp.where(present[None, :] & (rank[None, :] == number[:, None]), number[None, :], 0),
        axis=1,
    )
    count = jnp.sum(present.astype(jnp.int32))
    rank_of = jnp.sum(jnp.where(equal, rank[:, None], 0), axis=0)
    target = jnp.where(inside, rank_of * 128 + (ids & 127), -1)
    info = jnp.concatenate(
        [count[None], listed, jnp.zeros((BATCH,), jnp.int32)]
    ).astype(jnp.int32)
    rows = flat_ids.shape[0]
    shape = jax.ShapeDtypeStruct((width, rows // 2), jnp.bfloat16)
    return pl.pallas_call(
        pick_kernel,
        out_shape=(shape, shape),
        in_specs=[SMEM, ANY, VMEM],
        out_specs=(VMEM, VMEM),
        scratch_shapes=[
            pltpu.VMEM((2, width, BATCH * 128), jnp.bfloat16),
            pltpu.VMEM((width, rows), jnp.float32),
            pltpu.SemaphoreType.DMA((2, BATCH)),
        ],
        name="pick_rows",
    )(info, emb_t, target[None, :])


def norm_kernel(n, pos, gain, *refs):
    count = 2 * n - 1
    first = refs[:count]
    second = refs[count : 2 * count]
    out = refs[2 * count]
    raw, sems = refs[2 * count + 1 :]
    seq_index, tp_index = pos[0], pos[1]
    split = first[0].shape[1]
    more = second[0].shape[1]
    shifts = [0] + [d for k in range(1, n) for d in (-k, k)]

    def each(act):
        for i, shift in enumerate(shifts):
            quarter = tp_index + shift
            slot = lax.bitwise_xor(seq_index, jnp.clip(quarter, 0, n - 1))

            @pl.when((quarter >= 0) & (quarter < n))
            def _(i=i, slot=slot):
                act(
                    pltpu.make_async_copy(
                        first[i], raw.at[slot, :, pl.ds(0, split)], sems.at[0, i]
                    )
                )
                act(
                    pltpu.make_async_copy(
                        second[i], raw.at[slot, :, pl.ds(split, more)], sems.at[1, i]
                    )
                )

    each(lambda copy: copy.start())
    each(lambda copy: copy.wait())
    width, rows = raw.shape[1:]
    step = 128
    pieces = [(at, min(step, width - at)) for at in range(0, width, step)]

    def squares(r, total):
        for at, size in pieces:
            block = raw[r, at : at + size, :].astype(jnp.float32)
            total = total + jnp.sum((block * block).reshape(size // 8, 8, rows), axis=0)
        return total

    total = lax.fori_loop(0, n, squares, jnp.zeros((8, rows), jnp.float32))
    mean_sq = jnp.sum(total, axis=0, keepdims=True) / (n * width)
    scale = lax.rsqrt(mean_sq + eps_norm)

    def write(r, carry):
        quarter = lax.bitwise_xor(seq_index, r)
        for at, size in pieces:
            block = raw[r, at : at + size, :].astype(jnp.float32)
            block = block * scale * gain[quarter, at : at + size, :]
            out[r, :, at : at + size] = block.T.astype(jnp.bfloat16)
        return carry

    lax.fori_loop(0, n, write, 0)


def norm_rows(n, pos, gain, first, second):
    width = first[0].shape[0]
    rows = first[0].shape[1] + second[0].shape[1]
    return pl.pallas_call(
        functools.partial(norm_kernel, n),
        out_shape=jax.ShapeDtypeStruct((n, rows, width), jnp.bfloat16),
        in_specs=[SMEM, VMEM] + [ANY] * (len(first) + len(second)),
        out_specs=VMEM,
        scratch_shapes=[
            pltpu.VMEM((n, width, rows), jnp.bfloat16),
            pltpu.SemaphoreType.DMA((2, len(first))),
        ],
        name="norm_rows",
    )(pos, gain, *first, *second)


def piece_copies(grp, pieces, store, tile, size, sems):
    own, core, near, far = pieces
    columns = pl.ds(tile * size, size)
    rows = own.shape[0]
    at = 0
    for r, block in ((0, own), (1, core)):
        yield pltpu.make_async_copy(
            block.at[:, columns], store.at[r, :, columns], sems.at[tile, at]
        )
        at += 1
    part = rows // len(near)
    for r, group in ((2, near), (3, far)):
        for i, block in enumerate(group):
            side, chunk = i % 2, i // 2
            half = grp if side == 0 else 1 - grp
            start = pl.multiple_of(half * (rows // 2) + chunk * part, 16)
            yield pltpu.make_async_copy(
                block.at[:, columns],
                store.at[r, pl.ds(start, part), columns],
                sems.at[tile, at],
            )
            at += 1


def proj_kernel(normed_cols, tile, parts, pos, x, gain, cosine, sine, *refs):
    grp = pos[2]
    near = refs[2 : 2 + parts]
    far = refs[2 + parts : 2 + 2 * parts]
    out, store, sems = refs[2 + 2 * parts :]
    pieces = (refs[0], refs[1], near, far)
    columns = out.shape[1]
    head = gain.shape[1]
    for at in range(columns // tile):
        for copy in piece_copies(grp, pieces, store, at, tile, sems):
            copy.start()
    for at in range(columns // tile):
        for copy in piece_copies(grp, pieces, store, at, tile, sems):
            copy.wait()
        total = None
        for r in range(4):
            part = jnp.dot(
                x[r],
                store[r, :, at * tile : (at + 1) * tile],
                preferred_element_type=jnp.float32,
            )
            total = part if total is None else total + part
        for h in range(tile // head):
            value = total[:, h * head : (h + 1) * head]
            start = at * tile + h * head
            if start < normed_cols:
                mean_sq = jnp.mean(value * value, axis=-1, keepdims=True)
                value = value * lax.rsqrt(mean_sq + eps_norm) * gain[...]
                turned = pltpu.roll(value, head // 2, 1)
                value = value * cosine[...] + turned * sine[...]
            out[:, start : start + head] = value.astype(jnp.bfloat16)


def project(normed_cols, pos, x, gain, cosine, sine, pieces):
    own, core, near, far = pieces
    width, columns = own.shape
    tile = 256
    rows = x.shape[1]
    return pl.pallas_call(
        functools.partial(proj_kernel, normed_cols, tile, len(near)),
        out_shape=jax.ShapeDtypeStruct((rows, columns), jnp.bfloat16),
        in_specs=[SMEM] + [VMEM] * 4 + [ANY] * (2 + 2 * len(near)),
        out_specs=VMEM,
        scratch_shapes=[
            pltpu.VMEM((4, width, columns), jnp.bfloat16),
            pltpu.SemaphoreType.DMA((columns // tile, 2 + 2 * len(near))),
        ],
        name="project",
    )(pos, x, gain[None, :], cosine, sine, own, core, *near, *far)


def softmax_mix(scores, scale, values):
    top = jnp.max(scores, axis=-1, keepdims=True)
    weights = jnp.exp((scores - top) * scale)
    total = jnp.sum(weights, axis=-1, keepdims=True)
    weights = (weights / total).astype(jnp.bfloat16)
    return jnp.dot(weights, values, preferred_element_type=jnp.float32)


def attend_kernel(cont_len, pos, q, k0, k1, k2, k3, v0, v1, v2, v3, ck, cv, out):
    seq_index = pos[0]
    tokens = k0.shape[0]
    head = k0.shape[1]
    group = q.shape[1] // head
    scale = query_scalar ** (-0.5)
    contract = (((1,), (1,)), ((), ()))
    keys = [k0, k1, k2, k3]
    values = jnp.concatenate([v0[...], v1[...], v2[...], v3[...]], axis=0)
    q_own = jnp.concatenate(
        [q[:tokens, g * head : (g + 1) * head] for g in range(group)], axis=0
    )
    rows = group * tokens
    q_at = lax.rem(lax.broadcasted_iota(jnp.int32, (rows, tokens), 0), tokens)
    k_at = lax.broadcasted_iota(jnp.int32, (rows, tokens), 1)
    ahead = q_at - k_at
    blocks = []
    for r in range(4):
        gap = ahead + (seq_index - lax.bitwise_xor(seq_index, r)) * tokens
        score = lax.dot_general(
            q_own, keys[r][...], contract, preferred_element_type=jnp.float32
        )
        blocks.append(jnp.where((gap >= 0) & (gap < WINDOW), score, -1e30))
    mixed = softmax_mix(jnp.concatenate(blocks, axis=1), scale, values)
    for g in range(group):
        out[:tokens, g * head : (g + 1) * head] = mixed[
            g * tokens : (g + 1) * tokens
        ].astype(jnp.bfloat16)

    conts = ck.shape[0]
    q_cont = jnp.concatenate(
        [q[tokens:, g * head : (g + 1) * head] for g in range(group)], axis=0
    )
    rows = group * conts
    q_row = lax.rem(lax.broadcasted_iota(jnp.int32, (rows, tokens), 0), conts)
    spot = lax.rem(q_row, cont_len)
    k_at = lax.broadcasted_iota(jnp.int32, (rows, tokens), 1)
    blocks = []
    for r in range(4):
        base = lax.bitwise_xor(seq_index, r) * tokens - (4 * tokens - WINDOW)
        score = lax.dot_general(
            q_cont, keys[r][...], contract, preferred_element_type=jnp.float32
        )
        blocks.append(jnp.where(k_at + base > spot, score, -1e30))
    q_row = lax.rem(lax.broadcasted_iota(jnp.int32, (rows, conts), 0), conts)
    k_row = lax.broadcasted_iota(jnp.int32, (rows, conts), 1)
    same = (q_row // cont_len) == (k_row // cont_len)
    score = lax.dot_general(q_cont, ck[...], contract, preferred_element_type=jnp.float32)
    blocks.append(jnp.where(same & (k_row <= q_row), score, -1e30))
    mixed = softmax_mix(
        jnp.concatenate(blocks, axis=1), scale, jnp.concatenate([values, cv[...]], axis=0)
    )
    for g in range(group):
        out[tokens:, g * head : (g + 1) * head] = mixed[
            g * conts : (g + 1) * conts
        ].astype(jnp.bfloat16)


def attend_rows(cont_len, head, pos, queries, prompt_kv, cont_kv):
    rows, q_cols = queries.shape
    kv_heads = cont_kv.shape[1] // (2 * head)
    group = q_cols // head // kv_heads
    tokens = prompt_kv[0].shape[0]
    conts = cont_kv.shape[0]

    def column(size, shift):
        return pl.BlockSpec((size, head), lambda h, pos: (0, h + shift))

    wide = pl.BlockSpec((rows, group * head), lambda h, pos: (0, h))
    return pl.pallas_call(
        functools.partial(attend_kernel, cont_len),
        out_shape=jax.ShapeDtypeStruct((rows, q_cols), jnp.bfloat16),
        grid_spec=pltpu.PrefetchScalarGridSpec(
            num_scalar_prefetch=1,
            grid=(kv_heads,),
            in_specs=[wide]
            + [column(tokens, 0)] * 4
            + [column(tokens, kv_heads)] * 4
            + [column(conts, 0), column(conts, kv_heads)],
            out_specs=wide,
        ),
        name="attend_rows",
    )(pos, queries, *prompt_kv, *prompt_kv, cont_kv, cont_kv)


def out_kernel(parts, split, pos, mixed, *refs):
    seq_index, grp = pos[0], pos[2]
    near = refs[2 : 2 + parts]
    far = refs[2 + parts : 2 + 2 * parts]
    out_a, out_b, store, sems = refs[2 + 2 * parts :]
    pieces = (refs[0], refs[1], near, far)
    size = store.shape[2]
    copies = list(piece_copies(grp, pieces, store, 0, size, sems))
    for copy in copies:
        copy.start()
    groups = [[0], [1], list(range(2, 2 + parts)), list(range(2 + parts, 2 + 2 * parts))]
    for r in range(4):
        for i in groups[r]:
            copies[i].wait()
        slot = lax.bitwise_xor(seq_index, r)
        part = lax.dot_general(
            store[r],
            mixed[...],
            (((1,), (1,)), ((), ())),
            preferred_element_type=jnp.float32,
        ).astype(jnp.bfloat16)
        out_a[slot] = part[:, :split]
        out_b[slot] = part[:, split:]


def project_out(split, pos, mixed, pieces):
    own, core, near, far = pieces
    width, size = own.shape
    rows = mixed.shape[0]
    return pl.pallas_call(
        functools.partial(out_kernel, len(near), split),
        out_shape=(
            jax.ShapeDtypeStruct((4, width, split), jnp.bfloat16),
            jax.ShapeDtypeStruct((4, width, rows - split), jnp.bfloat16),
        ),
        in_specs=[SMEM, VMEM] + [ANY] * (2 + 2 * len(near)),
        out_specs=(VMEM, VMEM),
        scratch_shapes=[
            pltpu.VMEM((4, width, size), jnp.bfloat16),
            pltpu.SemaphoreType.DMA((1, 2 + 2 * len(near))),
        ],
        name="project_out",
    )(pos, mixed, own, core, *near, *far)


def line_gather(value, axis):
    count = lax.axis_size(axis)
    up = [(i, i + 1) for i in range(count - 1)]
    down = [(i + 1, i) for i in range(count - 1)]
    blocks = [value]
    a = b = value
    for _ in range(count - 1):
        a = lax.ppermute(a, axis, up)
        b = lax.ppermute(b, axis, down)
        blocks += [a, b]
    return blocks


def line_scatter(parts, axis):
    count = lax.axis_size(axis)
    index = lax.axis_index(axis)

    def block(at):
        return lax.dynamic_index_in_dim(parts, jnp.clip(at, 0, count - 1), 0, False)

    a = b = None
    for step in range(1, count):
        far = count - step
        send_a, send_b = block(index + far), block(index - far)
        if a is not None:
            send_a = (send_a.astype(jnp.float32) + a.astype(jnp.float32)).astype(jnp.bfloat16)
            send_b = (send_b.astype(jnp.float32) + b.astype(jnp.float32)).astype(jnp.bfloat16)
        a = lax.ppermute(send_a, axis, [(i, i + 1) for i in range(step)])
        b = lax.ppermute(send_b, axis, [(count - 1 - i, count - 2 - i) for i in range(step)])
    return (
        block(index).astype(jnp.float32) + a.astype(jnp.float32) + b.astype(jnp.float32)
    )


def total_over(value, axis):
    count = lax.axis_size(axis)
    total = value
    for by in range(1, count):
        total = total + lax.ppermute(value, axis, [(i, (i + by) % count) for i in range(count)])
    return total


def weight_pieces(weight, chunks):
    count = lax.axis_size("seq")
    grp = lax.axis_index("grp")
    core = [(i, i ^ 1) for i in range(count)]
    across = [(i, i ^ 2) for i in range(count)]
    half = weight.shape[0] // 2
    part = half // chunks
    near = []
    for i in range(chunks):
        mine = lax.dynamic_slice_in_dim(weight, grp * half + i * part, part)
        got = lax.ppermute(mine, "seq", across)
        near += [got, lax.ppermute(got, "grp", [(0, 1), (1, 0)])]
    far = [lax.ppermute(block, "seq", core) for block in near]
    return weight, lax.ppermute(weight, "seq", core), near, far


def on_device(
    prompt, cont_ids, embed, pre_gain, w_query, w_keyval, q_gain, k_gain, w_out, post_gain
):
    tok_rows, local_cols = prompt.shape
    n_seq = lax.axis_size("seq")
    n_tp = lax.axis_size("tp")
    seq_index = lax.axis_index("seq")
    tp_index = lax.axis_index("tp")
    full_width = local_cols * n_tp
    cont_count, cont_len = cont_ids.shape
    own_conts = cont_count // n_seq
    cont_rows = own_conts * cont_len
    core = [(i, i ^ 1) for i in range(n_seq)]
    across = [(i, i ^ 2) for i in range(n_seq)]
    pos = jnp.stack([seq_index, tp_index, lax.axis_index("grp")]).astype(jnp.int32)

    kv_pieces = weight_pieces(w_keyval.reshape(w_keyval.shape[0], -1), 2)
    q_pieces = weight_pieces(w_query, 2)
    out_pieces = weight_pieces(w_out.T, 2)

    prompt_t = prompt.T
    prompt_blocks = line_gather(prompt_t, "tp")

    ids = cont_ids.reshape(n_seq, cont_rows)
    order = [lax.dynamic_index_in_dim(ids, seq_index ^ r, 0, False) for r in (0, 2, 1, 3)]
    keep, give = pick_rows(embed.T, jnp.concatenate(order), seq_index * embed.shape[0])
    keep = keep + lax.ppermute(give, "seq", core)
    mine = keep[:, :cont_rows] + lax.ppermute(keep[:, cont_rows:], "seq", across)
    cont_t = (mine.astype(jnp.float32) * math.sqrt(full_width)).astype(jnp.bfloat16)
    cont_blocks = line_gather(cont_t, "tp")

    head_dim = q_gain.shape[0]
    positions = jnp.concatenate(
        [
            seq_index * tok_rows + jnp.arange(tok_rows, dtype=jnp.int32),
            n_seq * tok_rows + jnp.arange(cont_rows, dtype=jnp.int32) % cont_len,
        ]
    )
    half = head_dim // 2
    freqs = rope_base ** (
        -(jnp.arange(half, dtype=jnp.int32).astype(jnp.float32) * 2.0) / head_dim
    )
    angles = positions.astype(jnp.float32)[:, None] * freqs[None, :]
    cosine = jnp.cos(angles)
    sine = jnp.sin(angles)
    cosine = jnp.concatenate([cosine, cosine], axis=1)
    sine = jnp.concatenate([-sine, sine], axis=1)

    normed = norm_rows(
        n_tp, pos, pre_gain.reshape(n_tp, local_cols, 1), prompt_blocks, cont_blocks
    )
    kv_cols = w_keyval.shape[2]
    keyval = project(kv_cols, pos, normed, k_gain, cosine, sine, kv_pieces)
    prompt_kv = keyval[:tok_rows]
    cont_kv = keyval[tok_rows:]
    kv_core = lax.ppermute(prompt_kv, "seq", core)
    kv_near = lax.ppermute(prompt_kv, "seq", across)
    kv_far = lax.ppermute(kv_near, "seq", core)
    queries = project(w_query.shape[1], pos, normed, q_gain, cosine, sine, q_pieces)
    mixed = attend_rows(
        cont_len, head_dim, pos, queries, [prompt_kv, kv_core, kv_near, kv_far], cont_kv
    )
    part_p, part_c = project_out(tok_rows, pos, mixed, out_pieces)
    gain_part = lax.dynamic_slice_in_dim(post_gain, tp_index * local_cols, local_cols)[:, None]

    def finish(parts, rows_t):
        attn = line_scatter(parts, "tp")
        row_sq = total_over(jnp.sum(attn * attn, axis=0, keepdims=True), "tp")
        factor = lax.rsqrt(row_sq / full_width + eps_norm)
        return (rows_t.astype(jnp.float32) + attn * factor * gain_part).astype(jnp.bfloat16)

    prompt_out = finish(part_p, prompt_t).T
    cont_out = finish(part_c, cont_t).T
    return (prompt_out, cont_out.reshape(own_conts, cont_len, local_cols))


def solution(mesh):
    shape = mesh.shape
    paired = shape["grp"] == 2 and shape["seq"] == 4 and shape["tp"] == 4
    return jax.shard_map(
        on_device if paired else plain_device,
        mesh=mesh,
        in_specs=(
            P(("grp", "seq"), "tp"),
            P("grp", None),
            P("seq", "tp"),
            P(),
            P("seq", "tp"),
            P("seq", None, "tp"),
            P(),
            P(),
            P("tp", "seq"),
            P(),
        ),
        out_specs=(P(("grp", "seq"), "tp"), P(("grp", "seq"), None, "tp")),
        check_vma=False,
    )
```

```python
import functools
import math

import jax
import jax.numpy as jnp
from jax import lax
from jax.experimental import pallas as pl
from jax.experimental.pallas import tpu as pltpu
from jax.sharding import PartitionSpec as P


WINDOW = 1024


eps_norm = 1e-06
query_scalar = 168.0
rope_base = 10000.0


def from_behind(value, axis, by):
    count = lax.axis_size(axis)
    pairs = [(i, i + by) for i in range(count) if 0 <= i + by < count]
    return lax.ppermute(value, axis, pairs)


def from_root(value, axis, root):
    mine = lax.axis_index(axis) == root
    return lax.psum(jnp.where(mine, value, jnp.zeros_like(value)), axis)


def rms_scale(values, gain):
    mean_sq = jnp.mean(values * values, axis=-1, keepdims=True)
    return values * lax.rsqrt(mean_sq + eps_norm) * gain


def rotate(values, positions):
    half = values.shape[-1] // 2
    freqs = rope_base ** (
        -(jnp.arange(half, dtype=jnp.int32).astype(jnp.float32) * 2.0) / values.shape[-1]
    )
    angles = positions.astype(jnp.float32)[:, None] * freqs[None, :]
    cosine = jnp.cos(angles)[:, None, :]
    sine = jnp.sin(angles)[:, None, :]
    first = values[..., :half]
    second = values[..., half:]
    return jnp.concatenate(
        [first * cosine - second * sine, second * cosine + first * sine], axis=-1
    )


def attend(queries, keys, values, allowed):
    rows, heads, width = queries.shape
    kv_heads = keys.shape[1]
    grouped = queries.reshape(rows, kv_heads, heads // kv_heads, width)
    scores = jnp.einsum(
        "qkgd,nkd->kgqn", grouped, keys, preferred_element_type=jnp.float32
    ) * query_scalar ** (-0.5)
    scores = jnp.where(allowed[None, None], scores, -1e30)
    top = jnp.max(scores, axis=-1, keepdims=True)
    weights = jnp.exp(scores - top)
    weights = (weights / jnp.sum(weights, axis=-1, keepdims=True)).astype(jnp.bfloat16)
    mixed = jnp.einsum("kgqn,nkd->qkgd", weights, values, preferred_element_type=jnp.float32)
    return mixed.reshape(rows, heads * width).astype(jnp.bfloat16)


def plain_device(
    prompt, cont_ids, embed, pre_gain, w_query, w_keyval, q_gain, k_gain, w_out, post_gain
):
    tok_rows, local_cols = prompt.shape
    n_seq = lax.axis_size("seq")
    n_tp = lax.axis_size("tp")
    seq_index = lax.axis_index("seq")
    tp_index = lax.axis_index("tp")
    full_width = local_cols * n_tp
    cont_count, cont_len = cont_ids.shape
    own_conts = cont_count // n_seq
    cont_rows = own_conts * cont_len
    vocab_rows = embed.shape[0]
    flat_ids = cont_ids.reshape(-1)
    vocab_start = seq_index * vocab_rows
    chosen = flat_ids - vocab_start
    inside = (chosen >= 0) & (chosen < vocab_rows)
    picked = jnp.take(embed, jnp.clip(chosen, 0, vocab_rows - 1), axis=0)
    embedded = lax.psum_scatter(
        jnp.where(inside[:, None], picked.astype(jnp.float32), 0.0).astype(jnp.bfloat16),
        "seq",
        scatter_dimension=0,
        tiled=True,
    ).astype(jnp.float32)
    cont_x = (embedded * math.sqrt(full_width)).astype(jnp.bfloat16)
    rows_x = jnp.concatenate([prompt, cont_x], axis=0)
    whole = lax.all_gather(rows_x, "tp", axis=1, tiled=True)
    normed = rms_scale(whole.astype(jnp.float32), pre_gain).astype(jnp.bfloat16)
    all_rows = normed.shape[0]
    q_cols = w_query.shape[1]
    kv_cols = w_keyval.shape[2]
    query_part = jnp.dot(
        normed,
        lax.all_gather(w_query, "seq", axis=0, tiled=True),
        preferred_element_type=jnp.float32,
    )
    kv_part = jnp.einsum(
        "rd,dcf->rcf",
        normed,
        lax.all_gather(w_keyval, "seq", axis=0, tiled=True),
        preferred_element_type=jnp.float32,
    )
    head_dim = q_gain.shape[0]
    q_heads = q_cols // head_dim
    kv_heads = kv_cols // head_dim
    tokens_total = n_seq * tok_rows
    positions = jnp.concatenate(
        [
            seq_index * tok_rows + jnp.arange(tok_rows, dtype=jnp.int32),
            tokens_total + jnp.arange(cont_rows, dtype=jnp.int32) % cont_len,
        ]
    )
    queries = rotate(
        rms_scale(query_part.reshape(all_rows, q_heads, head_dim), q_gain), positions
    ).astype(jnp.bfloat16)
    keys = rotate(
        rms_scale(kv_part[:, 0].reshape(all_rows, kv_heads, head_dim), k_gain), positions
    ).astype(jnp.bfloat16)
    values = kv_part[:, 1].astype(jnp.bfloat16)
    keyval = jnp.stack([keys.reshape(all_rows, kv_cols), values], axis=1)
    prompt_kv = keyval[:tok_rows]
    cont_kv = keyval[tok_rows:]
    reach = WINDOW // tok_rows
    earlier = []
    moving = prompt_kv
    for _ in range(reach):
        moving = from_behind(moving, "seq", 1)
        earlier = [moving] + earlier
    band = jnp.concatenate(earlier + [prompt_kv], axis=0)
    q_pos = positions[:tok_rows]
    key_pos = seq_index * tok_rows - reach * tok_rows + jnp.arange(band.shape[0], dtype=jnp.int32)
    allowed = (
        (key_pos[None, :] <= q_pos[:, None])
        & (key_pos[None, :] > q_pos[:, None] - WINDOW)
        & (key_pos[None, :] >= 0)
    )
    prompt_mix = attend(
        queries[:tok_rows],
        band[:, 0].reshape(-1, kv_heads, head_dim),
        band[:, 1].reshape(-1, kv_heads, head_dim),
        allowed,
    )
    final = from_root(band[band.shape[0] - WINDOW :], "seq", n_seq - 1)
    spots = jnp.arange(cont_len, dtype=jnp.int32)
    allowed_cont = jnp.concatenate(
        [
            jnp.arange(WINDOW, dtype=jnp.int32)[None, :] > spots[:, None],
            spots[None, :] <= spots[:, None],
        ],
        axis=1,
    )
    cont_q = queries[tok_rows:].reshape(own_conts, cont_len, q_heads, head_dim)
    cont_keys = cont_kv.reshape(own_conts, cont_len, 2, kv_cols)

    def one_cont(query_block, key_block):
        joined = jnp.concatenate([final, key_block], axis=0)
        return attend(
            query_block,
            joined[:, 0].reshape(-1, kv_heads, head_dim),
            joined[:, 1].reshape(-1, kv_heads, head_dim),
            allowed_cont,
        )

    cont_mix = jax.vmap(one_cont)(cont_q, cont_keys).reshape(cont_rows, q_cols)
    mixed = jnp.concatenate([prompt_mix, cont_mix], axis=0)
    partial_rows = jnp.dot(
        mixed, lax.all_gather(w_out, "seq", axis=1, tiled=True), preferred_element_type=jnp.float32
    )
    attn_proj = lax.psum_scatter(
        partial_rows.astype(jnp.bfloat16), "tp", scatter_dimension=1, tiled=True
    ).astype(jnp.float32)
    row_sq = lax.psum(jnp.sum(attn_proj * attn_proj, axis=1), "tp")
    factor = lax.rsqrt(row_sq / full_width + eps_norm)
    gain_part = lax.dynamic_slice_in_dim(post_gain, tp_index * local_cols, local_cols)
    result = (rows_x.astype(jnp.float32) + attn_proj * factor[:, None] * gain_part).astype(
        jnp.bfloat16
    )
    return (result[:tok_rows], result[tok_rows:].reshape(own_conts, cont_len, local_cols))


ANY = pl.BlockSpec(memory_space=pl.ANY)
SMEM = pl.BlockSpec(memory_space=pltpu.SMEM)
VMEM = pl.BlockSpec(memory_space=pltpu.VMEM)
BATCH = 8


def pick_kernel(info, emb, lanes, listed, ids, out, buf, held, acc, sems):
    rounds = (info[0] + BATCH - 1) // BATCH
    width = BATCH * 128
    per_group = 128 // BATCH

    def copies(step, slot):
        for b in range(BATCH):
            block = info[1 + step * BATCH + b]
            yield pltpu.make_async_copy(
                emb.at[:, pl.ds(pl.multiple_of(block * 128, 128), 128)],
                buf.at[slot, :, pl.ds(b * 128, 128)],
                sems.at[slot, b],
            )

    acc[...] = jnp.zeros_like(acc)

    @pl.when(rounds > 0)
    def _():
        for copy in copies(0, 0):
            copy.start()

    def body(step, carry):
        slot = lax.rem(step, 2)
        group = step // per_group
        within = step - group * per_group

        @pl.when(step + 1 < rounds)
        def _():
            for copy in copies(step + 1, 1 - slot):
                copy.start()

        for copy in copies(step, slot):
            copy.wait()
        lane = lanes[pl.ds(group, 1), :]
        at = lax.broadcasted_iota(jnp.int32, lane.shape, 1) - within * BATCH
        rel = jnp.where((lane >= 0) & (at >= 0) & (at < BATCH), at * 128 + lane, -1)
        hot = lax.broadcasted_iota(jnp.int32, (width, 128), 0) == rel
        got = jnp.dot(buf[slot], hot.astype(jnp.bfloat16), preferred_element_type=jnp.float32)

        @pl.when(within == 0)
        def _():
            held[...] = got

        @pl.when(within > 0)
        def _():
            held[...] += got

        @pl.when((within == per_group - 1) | (step == rounds - 1))
        def _():
            name = listed[pl.ds(pl.multiple_of(group * 128, 128), 128), :]
            spread = (name == ids[...]).astype(jnp.bfloat16)
            acc[...] += jnp.dot(
                held[...].astype(jnp.bfloat16), spread, preferred_element_type=jnp.float32
            )

        return carry

    lax.fori_loop(0, rounds, body, 0)
    out[...] = acc[...].astype(jnp.bfloat16)


def pick_rows(emb_t, flat_ids, vocab_start):
    width, vocab = emb_t.shape
    rows = flat_ids.shape[0]
    ids = flat_ids - vocab_start
    ids = jnp.where((ids >= 0) & (ids < vocab), ids, -2)
    number = jnp.arange(rows, dtype=jnp.int32)
    same = (ids[:, None] == ids[None, :]) & (number[:, None] < number[None, :])
    first = (ids >= 0) & ~jnp.any(same, axis=0)
    rank = jnp.sum(
        jnp.where((number[:, None] < number[None, :]) & first[:, None], 1, 0), axis=0
    )
    listed = jnp.max(
        jnp.where(first[None, :] & (rank[None, :] == number[:, None]), ids[None, :], -1),
        axis=1,
    )
    count = jnp.sum(first.astype(jnp.int32))
    info = jnp.concatenate(
        [count[None], jnp.maximum(listed, 0) >> 7, jnp.zeros((BATCH,), jnp.int32)]
    )
    lanes = jnp.where(listed >= 0, listed & 127, -1).reshape(rows // 128, 128)
    return pl.pallas_call(
        pick_kernel,
        out_shape=jax.ShapeDtypeStruct((width, rows), jnp.bfloat16),
        in_specs=[SMEM, ANY, VMEM, VMEM, VMEM],
        out_specs=VMEM,
        scratch_shapes=[
            pltpu.VMEM((2, width, BATCH * 128), jnp.bfloat16),
            pltpu.VMEM((width, 128), jnp.float32),
            pltpu.VMEM((width, rows), jnp.float32),
            pltpu.SemaphoreType.DMA((2, BATCH)),
        ],
        name="pick_rows",
    )(info, emb_t, lanes, listed[:, None], ids[None, :])


def padded(width):
    return -(-width // 128) * 128


def norm_kernel(pos, gain, x, out):
    n, width, rows = x.shape
    pitch = padded(width)
    step = 128
    pieces = [(at, min(step, width - at)) for at in range(0, width, step)]

    def squares(r, total):
        for at, size in pieces:
            block = x[r, at : at + size, :].astype(jnp.float32)
            total = total + jnp.sum((block * block).reshape(size // 8, 8, rows), axis=0)
        return total

    total = lax.fori_loop(0, n, squares, jnp.zeros((8, rows), jnp.float32))
    mean_sq = jnp.sum(total, axis=0, keepdims=True) / (n * width)
    scale = lax.rsqrt(mean_sq + eps_norm)
    for r in range(n):
        for at, size in pieces:
            block = x[r, at : at + size, :].astype(jnp.float32) * scale
            block = block.T * gain[r : r + 1, at : at + size]
            out[:, r * pitch + at : r * pitch + at + size] = block.astype(jnp.bfloat16)


def norm_rows(pos, gain, x):
    n, width, rows = x.shape
    return pl.pallas_call(
        norm_kernel,
        out_shape=jax.ShapeDtypeStruct((rows, n * padded(width)), jnp.bfloat16),
        in_specs=[SMEM, VMEM, VMEM],
        out_specs=VMEM,
        name="norm_rows",
    )(pos, gain, x)


def piece_copies(grp, pieces, store, sems):
    own, core, near, far = pieces
    rows = own.shape[0]
    part = rows // len(near)
    groups = [
        [pltpu.make_async_copy(own, store.at[0], sems.at[0])],
        [pltpu.make_async_copy(core, store.at[1], sems.at[1])],
    ]
    at = 2
    for r, blocks in ((2, near), (3, far)):
        group = []
        for i, block in enumerate(blocks):
            half = grp if i % 2 == 0 else 1 - grp
            start = pl.multiple_of(half * (rows // 2) + (i // 2) * part, 16)
            group.append(
                pltpu.make_async_copy(block, store.at[r, pl.ds(start, part), :], sems.at[at])
            )
            at += 1
        groups.append(group)
    return groups


def proj_kernel(normed_cols, count, parts, pos, gain, cosine, sine, *refs):
    sources, refs = refs[:count], refs[count:]
    near, far = refs[2 : 2 + parts], refs[2 + parts : 2 + 2 * parts]
    out, x, store, total, x_sems, w_sems = refs[2 + 2 * parts :]
    groups = piece_copies(pos[2], (refs[0], refs[1], near, far), store, w_sems)
    width, pitch = store.shape[1], x.shape[2]
    loads = []
    for r in range(4):
        at = 0
        slot = pl.multiple_of(lax.bitwise_xor(pos[0], r) * pitch, 128)
        for i, source in enumerate(sources):
            rows = source.shape[0]
            loads.append(
                pltpu.make_async_copy(
                    source.at[:, pl.ds(slot, pitch)], x.at[r, pl.ds(at, rows), :], x_sems.at[r, i]
                )
            )
            loads[-1].start()
            at += rows
        for copy in groups[r]:
            copy.start()
    head = gain.shape[1]
    for r in range(4):
        for copy in loads[r * count : (r + 1) * count] + groups[r]:
            copy.wait()
        part = jnp.dot(x[r, :, :width], store[r], preferred_element_type=jnp.float32)
        if r == 0:
            total[...] = part
        else:
            total[...] += part
    for start in range(0, out.shape[1], head):
        value = total[:, start : start + head]
        if start < normed_cols:
            mean_sq = jnp.mean(value * value, axis=-1, keepdims=True)
            value = value * lax.rsqrt(mean_sq + eps_norm) * gain[...]
            turned = pltpu.roll(value, head // 2, 1)
            value = value * cosine[...] + turned * sine[...]
        out[:, start : start + head] = value.astype(jnp.bfloat16)


def project(normed_cols, pos, sources, gain, cosine, sine, pieces):
    own, core, near, far = pieces
    width, columns = own.shape
    rows = sum(source.shape[0] for source in sources)
    return pl.pallas_call(
        functools.partial(proj_kernel, normed_cols, len(sources), len(near)),
        out_shape=jax.ShapeDtypeStruct((rows, columns), jnp.bfloat16),
        in_specs=[SMEM] + [VMEM] * 3 + [ANY] * (len(sources) + 2 + 2 * len(near)),
        out_specs=VMEM,
        scratch_shapes=[
            pltpu.VMEM((4, rows, padded(width)), jnp.bfloat16),
            pltpu.VMEM((4, width, columns), jnp.bfloat16),
            pltpu.VMEM((rows, columns), jnp.float32),
            pltpu.SemaphoreType.DMA((4, len(sources))),
            pltpu.SemaphoreType.DMA((2 + 2 * len(near),)),
        ],
        name="project",
    )(pos, gain[None, :], cosine, sine, *sources, own, core, *near, *far)


def softmax_mix(scores, scale, values):
    top = jnp.max(scores, axis=-1, keepdims=True)
    weights = jnp.exp((scores - top) * scale)
    total = jnp.sum(weights, axis=-1, keepdims=True)
    weights = (weights / total).astype(jnp.bfloat16)
    return jnp.dot(weights, values, preferred_element_type=jnp.float32)


def stacked(source, head):
    count = source.shape[1] // head
    return jnp.concatenate([source[:, g * head : (g + 1) * head] for g in range(count)], axis=0)


def unstack(mixed, out, head):
    rows = out.shape[1]
    for g in range(out.shape[2] // head):
        out[0, :, g * head : (g + 1) * head] = mixed[g * rows : (g + 1) * rows].astype(
            jnp.bfloat16
        )


CONTRACT = (((1,), (1,)), ((), ()))


def prompt_kernel(pos, q, k0, k2, v0, v2, out):
    own_index = pos[0]
    block = lax.bitwise_xor(own_index, pl.program_id(1))
    tokens, head = q.shape[0], k0.shape[1]
    keys = [k0[:tokens], k0[tokens:], k2[:tokens], k2[tokens:]]
    q_own = stacked(q, head)
    rows = q_own.shape[0]
    q_at = lax.rem(lax.broadcasted_iota(jnp.int32, (rows, tokens), 0), tokens)
    ahead = q_at - lax.broadcasted_iota(jnp.int32, (rows, tokens), 1)
    blocks = []
    for r in range(4):
        gap = ahead + (block - lax.bitwise_xor(own_index, r)) * tokens
        score = lax.dot_general(q_own, keys[r], CONTRACT, preferred_element_type=jnp.float32)
        blocks.append(jnp.where((gap >= 0) & (gap < WINDOW), score, -1e30))
    values = jnp.concatenate([v0[...], v2[...]], axis=0)
    scale = query_scalar ** (-0.5)
    unstack(softmax_mix(jnp.concatenate(blocks, axis=1), scale, values), out, head)


def cont_kernel(cont_len, tokens, pos, q, k0, k2, v0, v2, ck, cv, out):
    own_index = pos[0]
    conts, head = q.shape[0], k0.shape[1]
    keys = [k0[:tokens], k0[tokens:], k2[:tokens], k2[tokens:]]
    q_cont = stacked(q, head)
    rows = q_cont.shape[0]
    q_row = lax.rem(lax.broadcasted_iota(jnp.int32, (rows, tokens), 0), conts)
    late = lax.broadcasted_iota(jnp.int32, (rows, tokens), 1) - lax.rem(q_row, cont_len)
    blocks = []
    for r in range(4):
        base = lax.bitwise_xor(own_index, r) * tokens - (4 * tokens - WINDOW)
        score = lax.dot_general(q_cont, keys[r], CONTRACT, preferred_element_type=jnp.float32)
        blocks.append(jnp.where(late + base > 0, score, -1e30))
    q_row = lax.rem(lax.broadcasted_iota(jnp.int32, (rows, conts), 0), conts)
    k_row = lax.broadcasted_iota(jnp.int32, (rows, conts), 1)
    same = (q_row // cont_len) == (k_row // cont_len)
    score = lax.dot_general(q_cont, ck[...], CONTRACT, preferred_element_type=jnp.float32)
    blocks.append(jnp.where(same & (k_row <= q_row), score, -1e30))
    values = jnp.concatenate([v0[...], v2[...], cv[...]], axis=0)
    scale = query_scalar ** (-0.5)
    unstack(softmax_mix(jnp.concatenate(blocks, axis=1), scale, values), out, head)


def attend_rows(kernel, head, pos, queries, here_kv, there_kv, cont_kv):
    rows, q_cols = queries.shape[0] // 2, queries.shape[1]
    span = here_kv.shape[0]
    kv_heads = here_kv.shape[1] // (2 * head)
    wide = q_cols // kv_heads

    def column(shift):
        return pl.BlockSpec((span, head), lambda h, b, pos: (0, h + shift))

    def cont_column(shift):
        return pl.BlockSpec((rows, head), lambda h, b, pos: (b, h + shift))

    specs = [pl.BlockSpec((rows, wide), lambda h, b, pos: (b, h))]
    specs += [column(0), column(0), column(kv_heads), column(kv_heads)]
    operands = [queries, here_kv, there_kv, here_kv, there_kv]
    if cont_kv is not None:
        specs += [cont_column(0), cont_column(kv_heads)]
        operands += [cont_kv, cont_kv]
    return pl.pallas_call(
        kernel,
        out_shape=jax.ShapeDtypeStruct((2, rows, q_cols), jnp.bfloat16),
        grid_spec=pltpu.PrefetchScalarGridSpec(
            num_scalar_prefetch=1,
            grid=(kv_heads, 2),
            in_specs=specs,
            out_specs=pl.BlockSpec((1, rows, wide), lambda h, b, pos: (b, 0, h)),
        ),
        name="attend_rows",
    )(pos, *operands)


def out_kernel(parts, pos, mine, theirs, *refs):
    seq_index, grp = pos[0], pos[2]
    core = lax.bitwise_and(seq_index, 1)
    near, far = refs[2 : 2 + parts], refs[2 + parts : 2 + 2 * parts]
    out, mixed, turned, store, m_sems, sems = refs[2 + 2 * parts :]
    groups = piece_copies(grp, (refs[0], refs[1], near, far), store, sems)
    half = mine.shape[1]
    loads = []
    for i, (source, side) in enumerate(((mine, core), (theirs, 1 - core))):
        columns = pl.ds(pl.multiple_of(side * half, 128), half)
        loads.append(pltpu.make_async_copy(source, mixed.at[:, columns], m_sems.at[i]))
        loads[i].start()
    for group in groups:
        for copy in group:
            copy.start()
    for copy in loads:
        copy.wait()
    turned[...] = mixed[...].T
    for r in range(4):
        for copy in groups[r]:
            copy.wait()
        slot = lax.bitwise_xor(seq_index, r)
        size = store.shape[1] // 4
        for at in range(0, store.shape[1], size):
            out[slot, at : at + size] = jnp.dot(
                store[r, at : at + size], turned[...], preferred_element_type=jnp.float32
            ).astype(jnp.bfloat16)


def project_out(pos, mine, theirs, pieces):
    own, core, near, far = pieces
    width, size = own.shape
    rows = mine.shape[0]
    return pl.pallas_call(
        functools.partial(out_kernel, len(near)),
        out_shape=jax.ShapeDtypeStruct((4, width, rows), jnp.bfloat16),
        in_specs=[SMEM] + [ANY] * (4 + 2 * len(near)),
        out_specs=VMEM,
        scratch_shapes=[
            pltpu.VMEM((rows, size), jnp.bfloat16),
            pltpu.VMEM((size, rows), jnp.bfloat16),
            pltpu.VMEM((4, width, size), jnp.bfloat16),
            pltpu.SemaphoreType.DMA((2,)),
            pltpu.SemaphoreType.DMA((2 + 2 * len(near),)),
        ],
        name="project_out",
    )(pos, mine, theirs, own, core, *near, *far)


def line_scatter(parts, axis):
    count = lax.axis_size(axis)
    index = lax.axis_index(axis)

    def block(at):
        return lax.dynamic_index_in_dim(parts, jnp.clip(at, 0, count - 1), 0, False)

    a = b = None
    for step in range(1, count):
        far = count - step
        send_a, send_b = block(index + far), block(index - far)
        if a is not None:
            send_a = (send_a.astype(jnp.float32) + a.astype(jnp.float32)).astype(jnp.bfloat16)
            send_b = (send_b.astype(jnp.float32) + b.astype(jnp.float32)).astype(jnp.bfloat16)
        a = lax.ppermute(send_a, axis, [(i, i + 1) for i in range(step)])
        b = lax.ppermute(send_b, axis, [(count - 1 - i, count - 2 - i) for i in range(step)])
    return (
        block(index).astype(jnp.float32) + a.astype(jnp.float32) + b.astype(jnp.float32)
    )


def total_over(value, axis):
    count = lax.axis_size(axis)
    total = value
    for by in range(1, count):
        pairs = [(i, (i + by) % count) for i in range(count)]
        total = total + lax.ppermute(value, axis, pairs)
    return total


def swap(by):
    return [(i, i ^ by) for i in range(lax.axis_size("seq"))]


ACROSS = [(0, 1), (1, 0)]


def half_pieces(mine, other):
    half = mine.shape[0] // 2
    start = lax.axis_index("grp") * half
    near = lax.ppermute(lax.dynamic_slice_in_dim(mine, start, half), "seq", swap(2))
    far = lax.ppermute(lax.dynamic_slice_in_dim(other, start, half), "seq", swap(3))
    core = lax.ppermute(other, "seq", swap(1))
    near_x = lax.ppermute(near, "grp", ACROSS)
    far_x = lax.ppermute(far, "grp", ACROSS)
    return mine, core, [near, near_x], [far, far_x]


def full_pieces(weight, chunks):
    half = weight.shape[0] // 2
    part = half // chunks
    near, far = [], []
    core = lax.ppermute(weight, "seq", swap(1))
    for i in range(chunks):
        start = lax.axis_index("grp") * half + i * part
        mine = lax.dynamic_slice_in_dim(weight, start, part)
        got = lax.ppermute(mine, "seq", swap(2))
        more = lax.ppermute(got, "grp", ACROSS)
        near += [got, more]
        far += [lax.ppermute(got, "seq", swap(1)), lax.ppermute(more, "seq", swap(1))]
    return weight, core, near, far


def on_device(*args):
    return paired_device(*args)


def paired_device(
    prompt, cont_ids, embed, pre_gain, w_query, w_keyval, q_gain, k_gain, w_out, post_gain
):
    tok_rows, local_cols = prompt.shape
    n_seq = lax.axis_size("seq")
    n_tp = lax.axis_size("tp")
    seq_index = lax.axis_index("seq")
    tp_index = lax.axis_index("tp")
    core_index = seq_index & 1
    full_width = local_cols * n_tp
    cont_count, cont_len = cont_ids.shape
    own_conts = cont_count // n_seq
    cont_rows = own_conts * cont_len
    head_dim = q_gain.shape[0]
    pos = jnp.stack([seq_index, tp_index, lax.axis_index("grp")]).astype(jnp.int32)

    prompt_t = prompt.T
    prompt_x = lax.all_gather(prompt_t, "tp", axis=0)

    def half_of(weight, side):
        size = weight.shape[-1] // 2
        part = lax.dynamic_slice_in_dim(weight, side * size, size, weight.ndim - 1)
        return part.reshape(part.shape[0], -1)

    kv_pieces = half_pieces(half_of(w_keyval, core_index), half_of(w_keyval, 1 - core_index))
    q_pieces = half_pieces(half_of(w_query, core_index), half_of(w_query, 1 - core_index))
    out_pieces = full_pieces(w_out.T, 2)

    ids = cont_ids.reshape(n_seq, cont_rows)
    held = []
    for parts in ((1, 3), (0, 2)):
        wanted = [lax.dynamic_index_in_dim(ids, seq_index ^ r, 0, False) for r in parts]
        start = seq_index * embed.shape[0]
        held.append(pick_rows(embed.T, jnp.concatenate(wanted), start))
    give, keep = held
    keep = keep + lax.ppermute(give, "seq", swap(1))
    mine = keep[:, :cont_rows] + lax.ppermute(keep[:, cont_rows:], "seq", swap(2))
    cont_t = (mine.astype(jnp.float32) * math.sqrt(full_width)).astype(jnp.bfloat16)
    cont_x = lax.all_gather(cont_t, "tp", axis=0)

    def turns(positions):
        lane = jnp.arange(head_dim, dtype=jnp.int32)
        half = head_dim // 2
        freqs = rope_base ** (-((lane % half).astype(jnp.float32) * 2.0) / head_dim)
        angles = positions.astype(jnp.float32)[:, None] * freqs[None, :]
        return jnp.cos(angles), jnp.sin(angles) * jnp.where(lane < half, -1.0, 1.0)

    row = jnp.arange(2 * tok_rows, dtype=jnp.int32)
    block = jnp.where(row < tok_rows, seq_index, seq_index ^ 1)
    prompt_turns = turns(block * tok_rows + row % tok_rows)
    spot = jnp.arange(2 * cont_rows, dtype=jnp.int32) % cont_len
    cont_turns = turns(n_seq * tok_rows + spot)

    gain = pre_gain.reshape(n_tp, local_cols)
    kv_cols = w_keyval.shape[2] // 2
    q_cols = w_query.shape[1] // 2

    def rows_of(x):
        normed = norm_rows(pos, gain, x)
        return [normed, lax.ppermute(normed, "seq", swap(1))]

    def shares(mixed):
        return mixed[0], lax.ppermute(mixed[1], "seq", swap(1))

    rows_p = rows_of(prompt_x)
    here_kv = project(kv_cols, pos, rows_p, k_gain, *prompt_turns, kv_pieces)
    there_kv = lax.ppermute(here_kv, "seq", swap(2))
    queries_p = project(q_cols, pos, rows_p, q_gain, *prompt_turns, q_pieces)
    mixed_p = attend_rows(prompt_kernel, head_dim, pos, queries_p, here_kv, there_kv, None)
    pair_p = shares(mixed_p)
    rows_c = rows_of(cont_x)
    cont_kv = project(kv_cols, pos, rows_c, k_gain, *cont_turns, kv_pieces)
    queries_c = project(q_cols, pos, rows_c, q_gain, *cont_turns, q_pieces)
    kernel = functools.partial(cont_kernel, cont_len, tok_rows)
    mixed_c = attend_rows(kernel, head_dim, pos, queries_c, here_kv, there_kv, cont_kv)
    pair_c = shares(mixed_c)
    part_p = project_out(pos, *pair_p, out_pieces)
    part_c = project_out(pos, *pair_c, out_pieces)
    gain_part = lax.dynamic_slice_in_dim(post_gain, tp_index * local_cols, local_cols)[:, None]

    attn_p = lax.psum_scatter(part_p, "tp", scatter_dimension=0).astype(jnp.float32)
    attn_c = line_scatter(part_c, "tp")
    row_sq = jnp.concatenate(
        [jnp.sum(attn * attn, axis=0, keepdims=True) for attn in (attn_p, attn_c)], axis=1
    )
    factor = lax.rsqrt(total_over(row_sq, "tp") / full_width + eps_norm)

    def finish(attn, factor, rows_t):
        return (rows_t.astype(jnp.float32) + attn * factor * gain_part).astype(jnp.bfloat16)

    prompt_out = finish(attn_p, factor[:, :tok_rows], prompt_t).T
    cont_out = finish(attn_c, factor[:, tok_rows:], cont_t).T
    return (prompt_out, cont_out.reshape(own_conts, cont_len, local_cols))


def solution(mesh):
    shape = mesh.shape
    paired = shape["grp"] == 2 and shape["seq"] == 4 and shape["tp"] == 4
    return jax.shard_map(
        on_device if paired else plain_device,
        mesh=mesh,
        in_specs=(
            P(("grp", "seq"), "tp"),
            P("grp", None),
            P("seq", "tp"),
            P(),
            P("seq", "tp"),
            P("seq", None, "tp"),
            P(),
            P(),
            P("tp", "seq"),
            P(),
        ),
        out_specs=(P(("grp", "seq"), "tp"), P(("grp", "seq"), None, "tp")),
        check_vma=False,
    )
```

```python
import functools
import math

import jax
import jax.numpy as jnp
from jax import lax
from jax.experimental import pallas as pl
from jax.experimental.pallas import tpu as pltpu
from jax.sharding import PartitionSpec as P


WINDOW = 1024


eps_norm = 1e-06
query_scalar = 168.0
rope_base = 10000.0


def from_behind(value, axis, by):
    count = lax.axis_size(axis)
    pairs = [(i, i + by) for i in range(count) if 0 <= i + by < count]
    return lax.ppermute(value, axis, pairs)


def from_root(value, axis, root):
    mine = lax.axis_index(axis) == root
    return lax.psum(jnp.where(mine, value, jnp.zeros_like(value)), axis)


def rms_scale(values, gain):
    mean_sq = jnp.mean(values * values, axis=-1, keepdims=True)
    return values * lax.rsqrt(mean_sq + eps_norm) * gain


def rotate(values, positions):
    half = values.shape[-1] // 2
    freqs = rope_base ** (
        -(jnp.arange(half, dtype=jnp.int32).astype(jnp.float32) * 2.0) / values.shape[-1]
    )
    angles = positions.astype(jnp.float32)[:, None] * freqs[None, :]
    cosine = jnp.cos(angles)[:, None, :]
    sine = jnp.sin(angles)[:, None, :]
    first = values[..., :half]
    second = values[..., half:]
    return jnp.concatenate(
        [first * cosine - second * sine, second * cosine + first * sine], axis=-1
    )


def attend(queries, keys, values, allowed):
    rows, heads, width = queries.shape
    kv_heads = keys.shape[1]
    grouped = queries.reshape(rows, kv_heads, heads // kv_heads, width)
    scores = jnp.einsum(
        "qkgd,nkd->kgqn", grouped, keys, preferred_element_type=jnp.float32
    ) * query_scalar ** (-0.5)
    scores = jnp.where(allowed[None, None], scores, -1e30)
    top = jnp.max(scores, axis=-1, keepdims=True)
    weights = jnp.exp(scores - top)
    weights = (weights / jnp.sum(weights, axis=-1, keepdims=True)).astype(jnp.bfloat16)
    mixed = jnp.einsum("kgqn,nkd->qkgd", weights, values, preferred_element_type=jnp.float32)
    return mixed.reshape(rows, heads * width).astype(jnp.bfloat16)


def plain_device(
    prompt, cont_ids, embed, pre_gain, w_query, w_keyval, q_gain, k_gain, w_out, post_gain
):
    tok_rows, local_cols = prompt.shape
    n_seq = lax.axis_size("seq")
    n_tp = lax.axis_size("tp")
    seq_index = lax.axis_index("seq")
    tp_index = lax.axis_index("tp")
    full_width = local_cols * n_tp
    cont_count, cont_len = cont_ids.shape
    own_conts = cont_count // n_seq
    cont_rows = own_conts * cont_len
    vocab_rows = embed.shape[0]
    flat_ids = cont_ids.reshape(-1)
    vocab_start = seq_index * vocab_rows
    chosen = flat_ids - vocab_start
    inside = (chosen >= 0) & (chosen < vocab_rows)
    picked = jnp.take(embed, jnp.clip(chosen, 0, vocab_rows - 1), axis=0)
    embedded = lax.psum_scatter(
        jnp.where(inside[:, None], picked.astype(jnp.float32), 0.0).astype(jnp.bfloat16),
        "seq",
        scatter_dimension=0,
        tiled=True,
    ).astype(jnp.float32)
    cont_x = (embedded * math.sqrt(full_width)).astype(jnp.bfloat16)
    rows_x = jnp.concatenate([prompt, cont_x], axis=0)
    whole = lax.all_gather(rows_x, "tp", axis=1, tiled=True)
    normed = rms_scale(whole.astype(jnp.float32), pre_gain).astype(jnp.bfloat16)
    all_rows = normed.shape[0]
    q_cols = w_query.shape[1]
    kv_cols = w_keyval.shape[2]
    query_part = jnp.dot(
        normed,
        lax.all_gather(w_query, "seq", axis=0, tiled=True),
        preferred_element_type=jnp.float32,
    )
    kv_part = jnp.einsum(
        "rd,dcf->rcf",
        normed,
        lax.all_gather(w_keyval, "seq", axis=0, tiled=True),
        preferred_element_type=jnp.float32,
    )
    head_dim = q_gain.shape[0]
    q_heads = q_cols // head_dim
    kv_heads = kv_cols // head_dim
    tokens_total = n_seq * tok_rows
    positions = jnp.concatenate(
        [
            seq_index * tok_rows + jnp.arange(tok_rows, dtype=jnp.int32),
            tokens_total + jnp.arange(cont_rows, dtype=jnp.int32) % cont_len,
        ]
    )
    queries = rotate(
        rms_scale(query_part.reshape(all_rows, q_heads, head_dim), q_gain), positions
    ).astype(jnp.bfloat16)
    keys = rotate(
        rms_scale(kv_part[:, 0].reshape(all_rows, kv_heads, head_dim), k_gain), positions
    ).astype(jnp.bfloat16)
    values = kv_part[:, 1].astype(jnp.bfloat16)
    keyval = jnp.stack([keys.reshape(all_rows, kv_cols), values], axis=1)
    prompt_kv = keyval[:tok_rows]
    cont_kv = keyval[tok_rows:]
    reach = WINDOW // tok_rows
    earlier = []
    moving = prompt_kv
    for _ in range(reach):
        moving = from_behind(moving, "seq", 1)
        earlier = [moving] + earlier
    band = jnp.concatenate(earlier + [prompt_kv], axis=0)
    q_pos = positions[:tok_rows]
    key_pos = seq_index * tok_rows - reach * tok_rows + jnp.arange(band.shape[0], dtype=jnp.int32)
    allowed = (
        (key_pos[None, :] <= q_pos[:, None])
        & (key_pos[None, :] > q_pos[:, None] - WINDOW)
        & (key_pos[None, :] >= 0)
    )
    prompt_mix = attend(
        queries[:tok_rows],
        band[:, 0].reshape(-1, kv_heads, head_dim),
        band[:, 1].reshape(-1, kv_heads, head_dim),
        allowed,
    )
    final = from_root(band[band.shape[0] - WINDOW :], "seq", n_seq - 1)
    spots = jnp.arange(cont_len, dtype=jnp.int32)
    allowed_cont = jnp.concatenate(
        [
            jnp.arange(WINDOW, dtype=jnp.int32)[None, :] > spots[:, None],
            spots[None, :] <= spots[:, None],
        ],
        axis=1,
    )
    cont_q = queries[tok_rows:].reshape(own_conts, cont_len, q_heads, head_dim)
    cont_keys = cont_kv.reshape(own_conts, cont_len, 2, kv_cols)

    def one_cont(query_block, key_block):
        joined = jnp.concatenate([final, key_block], axis=0)
        return attend(
            query_block,
            joined[:, 0].reshape(-1, kv_heads, head_dim),
            joined[:, 1].reshape(-1, kv_heads, head_dim),
            allowed_cont,
        )

    cont_mix = jax.vmap(one_cont)(cont_q, cont_keys).reshape(cont_rows, q_cols)
    mixed = jnp.concatenate([prompt_mix, cont_mix], axis=0)
    partial_rows = jnp.dot(
        mixed, lax.all_gather(w_out, "seq", axis=1, tiled=True), preferred_element_type=jnp.float32
    )
    attn_proj = lax.psum_scatter(
        partial_rows.astype(jnp.bfloat16), "tp", scatter_dimension=1, tiled=True
    ).astype(jnp.float32)
    row_sq = lax.psum(jnp.sum(attn_proj * attn_proj, axis=1), "tp")
    factor = lax.rsqrt(row_sq / full_width + eps_norm)
    gain_part = lax.dynamic_slice_in_dim(post_gain, tp_index * local_cols, local_cols)
    result = (rows_x.astype(jnp.float32) + attn_proj * factor[:, None] * gain_part).astype(
        jnp.bfloat16
    )
    return (result[:tok_rows], result[tok_rows:].reshape(own_conts, cont_len, local_cols))


ANY = pl.BlockSpec(memory_space=pl.ANY)
SMEM = pl.BlockSpec(memory_space=pltpu.SMEM)
VMEM = pl.BlockSpec(memory_space=pltpu.VMEM)
BATCH = 8


def pick_kernel(info, emb, lanes, listed, ids, out, buf, held, acc, sems):
    rounds = (info[0] + BATCH - 1) // BATCH
    width = BATCH * 128
    per_group = 128 // BATCH

    def copies(step, slot):
        for b in range(BATCH):
            block = info[1 + step * BATCH + b]
            yield pltpu.make_async_copy(
                emb.at[:, pl.ds(pl.multiple_of(block * 128, 128), 128)],
                buf.at[slot, :, pl.ds(b * 128, 128)],
                sems.at[slot, b],
            )

    acc[...] = jnp.zeros_like(acc)
    held[...] = jnp.zeros_like(held)

    @pl.when(rounds > 0)
    def _():
        for copy in copies(0, 0):
            copy.start()

    def body(step, carry):
        slot = lax.rem(step, 2)
        group = step // per_group
        within = step - group * per_group

        @pl.when(step + 1 < rounds)
        def _():
            for copy in copies(step + 1, 1 - slot):
                copy.start()

        for copy in copies(step, slot):
            copy.wait()
        lane = lanes[pl.ds(group, 1), :]
        at = lax.broadcasted_iota(jnp.int32, lane.shape, 1) - within * BATCH
        rel = jnp.where((lane >= 0) & (at >= 0) & (at < BATCH), at * 128 + lane, -1)
        hot = lax.broadcasted_iota(jnp.int32, (width, 128), 0) == rel
        hot = hot.astype(jnp.bfloat16)
        size = held.shape[0] // 4
        keep = jnp.where(within == 0, 0.0, 1.0)
        for start in range(0, held.shape[0], size):
            span = pl.ds(start, size)
            got = jnp.dot(buf[slot, span, :], hot, preferred_element_type=jnp.float32)
            held[span, :] = held[span, :] * keep + got

        @pl.when((within == per_group - 1) | (step == rounds - 1))
        def _():
            name = listed[pl.ds(pl.multiple_of(group * 128, 128), 128), :]
            spread = (name == ids[...]).astype(jnp.bfloat16)
            acc[...] += jnp.dot(
                held[...].astype(jnp.bfloat16), spread, preferred_element_type=jnp.float32
            )

        return carry

    lax.fori_loop(0, rounds, body, 0)
    out[...] = acc[...].astype(jnp.bfloat16)


def pick_rows(emb_t, flat_ids, vocab_start):
    width, vocab = emb_t.shape
    rows = flat_ids.shape[0]
    ids = flat_ids - vocab_start
    ids = jnp.where((ids >= 0) & (ids < vocab), ids, -2)
    number = jnp.arange(rows, dtype=jnp.int32)
    same = (ids[:, None] == ids[None, :]) & (number[:, None] < number[None, :])
    first = (ids >= 0) & ~jnp.any(same, axis=0)
    rank = jnp.sum(
        jnp.where((number[:, None] < number[None, :]) & first[:, None], 1, 0), axis=0
    )
    listed = jnp.max(
        jnp.where(first[None, :] & (rank[None, :] == number[:, None]), ids[None, :], -1),
        axis=1,
    )
    count = jnp.sum(first.astype(jnp.int32))
    info = jnp.concatenate(
        [count[None], jnp.maximum(listed, 0) >> 7, jnp.zeros((BATCH,), jnp.int32)]
    )
    lanes = jnp.where(listed >= 0, listed & 127, -1).reshape(rows // 128, 128)
    return pl.pallas_call(
        pick_kernel,
        out_shape=jax.ShapeDtypeStruct((width, rows), jnp.bfloat16),
        in_specs=[SMEM, ANY, VMEM, VMEM, VMEM],
        out_specs=VMEM,
        scratch_shapes=[
            pltpu.VMEM((2, width, BATCH * 128), jnp.bfloat16),
            pltpu.VMEM((width, 128), jnp.float32),
            pltpu.VMEM((width, rows), jnp.float32),
            pltpu.SemaphoreType.DMA((2, BATCH)),
        ],
        name="pick_rows",
    )(info, emb_t, lanes, listed[:, None], ids[None, :])


def padded(width):
    return -(-width // 128) * 128


def norm_kernel(pos, gain, x, out):
    n, width, rows = x.shape
    pitch = padded(width)
    step = 128
    pieces = [(at, min(step, width - at)) for at in range(0, width, step)]

    def squares(r, total):
        for at, size in pieces:
            block = x[r, at : at + size, :].astype(jnp.float32)
            total = total + jnp.sum((block * block).reshape(size // 8, 8, rows), axis=0)
        return total

    total = lax.fori_loop(0, n, squares, jnp.zeros((8, rows), jnp.float32))
    mean_sq = jnp.sum(total, axis=0, keepdims=True) / (n * width)
    scale = lax.rsqrt(mean_sq + eps_norm)
    for r in range(n):
        for at, size in pieces:
            block = x[r, at : at + size, :].astype(jnp.float32) * scale
            block = block.T * gain[r : r + 1, at : at + size]
            out[:, r * pitch + at : r * pitch + at + size] = block.astype(jnp.bfloat16)


def norm_rows(pos, gain, x):
    n, width, rows = x.shape
    return pl.pallas_call(
        norm_kernel,
        out_shape=jax.ShapeDtypeStruct((rows, n * padded(width)), jnp.bfloat16),
        in_specs=[SMEM, VMEM, VMEM],
        out_specs=VMEM,
        name="norm_rows",
    )(pos, gain, x)


def piece_copies(grp, pieces, store, sems):
    own, core, near, far = pieces
    rows = own.shape[0]
    part = rows // len(near)
    groups = [
        [pltpu.make_async_copy(own, store.at[0], sems.at[0])],
        [pltpu.make_async_copy(core, store.at[1], sems.at[1])],
    ]
    at = 2
    for r, blocks in ((2, near), (3, far)):
        group = []
        for i, block in enumerate(blocks):
            half = grp if i % 2 == 0 else 1 - grp
            start = pl.multiple_of(half * (rows // 2) + (i // 2) * part, 16)
            group.append(
                pltpu.make_async_copy(block, store.at[r, pl.ds(start, part), :], sems.at[at])
            )
            at += 1
        groups.append(group)
    return groups


def proj_kernel(normed_cols, count, parts, pos, gain, cosine, sine, *refs):
    sources, refs = refs[:count], refs[count:]
    near, far = refs[2 : 2 + parts], refs[2 + parts : 2 + 2 * parts]
    out, x, store, total, x_sems, w_sems = refs[2 + 2 * parts :]
    groups = piece_copies(pos[2], (refs[0], refs[1], near, far), store, w_sems)
    width, pitch = store.shape[1], x.shape[2]
    loads = []
    for r in range(4):
        at = 0
        slot = pl.multiple_of(lax.bitwise_xor(pos[0], r) * pitch, 128)
        for i, source in enumerate(sources):
            rows = source.shape[0]
            loads.append(
                pltpu.make_async_copy(
                    source.at[:, pl.ds(slot, pitch)], x.at[r, pl.ds(at, rows), :], x_sems.at[r, i]
                )
            )
            loads[-1].start()
            at += rows
        for copy in groups[r]:
            copy.start()
    head = gain.shape[1]
    for r in range(4):
        for copy in loads[r * count : (r + 1) * count] + groups[r]:
            copy.wait()
        part = jnp.dot(x[r, :, :width], store[r], preferred_element_type=jnp.float32)
        if r == 0:
            total[...] = part
        else:
            total[...] += part
    for start in range(0, out.shape[1], head):
        value = total[:, start : start + head]
        if start < normed_cols:
            mean_sq = jnp.mean(value * value, axis=-1, keepdims=True)
            value = value * lax.rsqrt(mean_sq + eps_norm) * gain[...]
            turned = pltpu.roll(value, head // 2, 1)
            value = value * cosine[...] + turned * sine[...]
        out[:, start : start + head] = value.astype(jnp.bfloat16)


def project(normed_cols, pos, sources, gain, cosine, sine, pieces):
    own, core, near, far = pieces
    width, columns = own.shape
    rows = sum(source.shape[0] for source in sources)
    return pl.pallas_call(
        functools.partial(proj_kernel, normed_cols, len(sources), len(near)),
        out_shape=jax.ShapeDtypeStruct((rows, columns), jnp.bfloat16),
        in_specs=[SMEM] + [VMEM] * 3 + [ANY] * (len(sources) + 2 + 2 * len(near)),
        out_specs=VMEM,
        scratch_shapes=[
            pltpu.VMEM((4, rows, padded(width)), jnp.bfloat16),
            pltpu.VMEM((4, width, columns), jnp.bfloat16),
            pltpu.VMEM((rows, columns), jnp.float32),
            pltpu.SemaphoreType.DMA((4, len(sources))),
            pltpu.SemaphoreType.DMA((2 + 2 * len(near),)),
        ],
        name="project",
    )(pos, gain[None, :], cosine, sine, *sources, own, core, *near, *far)


def softmax_mix(scores, scale, values):
    top = jnp.max(scores, axis=-1, keepdims=True)
    weights = jnp.exp((scores - top) * scale)
    total = jnp.sum(weights, axis=-1, keepdims=True)
    weights = (weights / total).astype(jnp.bfloat16)
    return jnp.dot(weights, values, preferred_element_type=jnp.float32)


def stacked(source, head):
    count = source.shape[1] // head
    return jnp.concatenate([source[:, g * head : (g + 1) * head] for g in range(count)], axis=0)


def unstack(mixed, out, head):
    rows = out.shape[1]
    for g in range(out.shape[2] // head):
        out[0, :, g * head : (g + 1) * head] = mixed[g * rows : (g + 1) * rows].astype(
            jnp.bfloat16
        )


CONTRACT = (((1,), (1,)), ((), ()))


def prompt_kernel(pos, q, k0, k2, v0, v2, out):
    own_index = pos[0]
    block = lax.bitwise_xor(own_index, pl.program_id(1))
    tokens, head = q.shape[0], k0.shape[1]
    keys = [k0[:tokens], k0[tokens:], k2[:tokens], k2[tokens:]]
    q_own = stacked(q, head)
    rows = q_own.shape[0]
    q_at = lax.rem(lax.broadcasted_iota(jnp.int32, (rows, tokens), 0), tokens)
    ahead = q_at - lax.broadcasted_iota(jnp.int32, (rows, tokens), 1)
    blocks = []
    for r in range(4):
        gap = ahead + (block - lax.bitwise_xor(own_index, r)) * tokens
        score = lax.dot_general(q_own, keys[r], CONTRACT, preferred_element_type=jnp.float32)
        blocks.append(jnp.where((gap >= 0) & (gap < WINDOW), score, -1e30))
    values = jnp.concatenate([v0[...], v2[...]], axis=0)
    scale = query_scalar ** (-0.5)
    unstack(softmax_mix(jnp.concatenate(blocks, axis=1), scale, values), out, head)


def cont_kernel(cont_len, tokens, pos, q, k0, k2, v0, v2, ck, cv, out):
    own_index = pos[0]
    conts, head = q.shape[0], k0.shape[1]
    keys = [k0[:tokens], k0[tokens:], k2[:tokens], k2[tokens:]]
    q_cont = stacked(q, head)
    rows = q_cont.shape[0]
    q_row = lax.rem(lax.broadcasted_iota(jnp.int32, (rows, tokens), 0), conts)
    late = lax.broadcasted_iota(jnp.int32, (rows, tokens), 1) - lax.rem(q_row, cont_len)
    blocks = []
    for r in range(4):
        base = lax.bitwise_xor(own_index, r) * tokens - (4 * tokens - WINDOW)
        score = lax.dot_general(q_cont, keys[r], CONTRACT, preferred_element_type=jnp.float32)
        blocks.append(jnp.where(late + base > 0, score, -1e30))
    q_row = lax.rem(lax.broadcasted_iota(jnp.int32, (rows, conts), 0), conts)
    k_row = lax.broadcasted_iota(jnp.int32, (rows, conts), 1)
    same = (q_row // cont_len) == (k_row // cont_len)
    score = lax.dot_general(q_cont, ck[...], CONTRACT, preferred_element_type=jnp.float32)
    blocks.append(jnp.where(same & (k_row <= q_row), score, -1e30))
    values = jnp.concatenate([v0[...], v2[...], cv[...]], axis=0)
    scale = query_scalar ** (-0.5)
    unstack(softmax_mix(jnp.concatenate(blocks, axis=1), scale, values), out, head)


def attend_rows(kernel, head, pos, queries, here_kv, there_kv, cont_kv):
    rows, q_cols = queries.shape[0] // 2, queries.shape[1]
    span = here_kv.shape[0]
    kv_heads = here_kv.shape[1] // (2 * head)
    wide = q_cols // kv_heads

    def column(shift):
        return pl.BlockSpec((span, head), lambda h, b, pos: (0, h + shift))

    def cont_column(shift):
        return pl.BlockSpec((rows, head), lambda h, b, pos: (b, h + shift))

    specs = [pl.BlockSpec((rows, wide), lambda h, b, pos: (b, h))]
    specs += [column(0), column(0), column(kv_heads), column(kv_heads)]
    operands = [queries, here_kv, there_kv, here_kv, there_kv]
    if cont_kv is not None:
        specs += [cont_column(0), cont_column(kv_heads)]
        operands += [cont_kv, cont_kv]
    return pl.pallas_call(
        kernel,
        out_shape=jax.ShapeDtypeStruct((2, rows, q_cols), jnp.bfloat16),
        grid_spec=pltpu.PrefetchScalarGridSpec(
            num_scalar_prefetch=1,
            grid=(kv_heads, 2),
            in_specs=specs,
            out_specs=pl.BlockSpec((1, rows, wide), lambda h, b, pos: (b, 0, h)),
        ),
        name="attend_rows",
    )(pos, *operands)


def out_kernel(parts, pos, mine, theirs, *refs):
    seq_index, grp = pos[0], pos[2]
    core = lax.bitwise_and(seq_index, 1)
    near, far = refs[2 : 2 + parts], refs[2 + parts : 2 + 2 * parts]
    out, mixed, turned, store, m_sems, sems = refs[2 + 2 * parts :]
    groups = piece_copies(grp, (refs[0], refs[1], near, far), store, sems)
    half = mine.shape[1]
    loads = []
    for i, (source, side) in enumerate(((mine, core), (theirs, 1 - core))):
        columns = pl.ds(pl.multiple_of(side * half, 128), half)
        loads.append(pltpu.make_async_copy(source, mixed.at[:, columns], m_sems.at[i]))
        loads[i].start()
    for group in groups:
        for copy in group:
            copy.start()
    for copy in loads:
        copy.wait()
    turned[...] = mixed[...].T
    for r in range(4):
        for copy in groups[r]:
            copy.wait()
        slot = lax.bitwise_xor(seq_index, r)
        size = store.shape[1] // 4
        for at in range(0, store.shape[1], size):
            out[slot, at : at + size] = jnp.dot(
                store[r, at : at + size], turned[...], preferred_element_type=jnp.float32
            ).astype(jnp.bfloat16)


def project_out(pos, mine, theirs, pieces):
    own, core, near, far = pieces
    width, size = own.shape
    rows = mine.shape[0]
    return pl.pallas_call(
        functools.partial(out_kernel, len(near)),
        out_shape=jax.ShapeDtypeStruct((4, width, rows), jnp.bfloat16),
        in_specs=[SMEM] + [ANY] * (4 + 2 * len(near)),
        out_specs=VMEM,
        scratch_shapes=[
            pltpu.VMEM((rows, size), jnp.bfloat16),
            pltpu.VMEM((size, rows), jnp.bfloat16),
            pltpu.VMEM((4, width, size), jnp.bfloat16),
            pltpu.SemaphoreType.DMA((2,)),
            pltpu.SemaphoreType.DMA((2 + 2 * len(near),)),
        ],
        name="project_out",
    )(pos, mine, theirs, own, core, *near, *far)


def line_scatter(parts, axis):
    count = lax.axis_size(axis)
    index = lax.axis_index(axis)

    def block(at):
        return lax.dynamic_index_in_dim(parts, jnp.clip(at, 0, count - 1), 0, False)

    a = b = None
    for step in range(1, count):
        far = count - step
        send_a, send_b = block(index + far), block(index - far)
        if a is not None:
            send_a = (send_a.astype(jnp.float32) + a.astype(jnp.float32)).astype(jnp.bfloat16)
            send_b = (send_b.astype(jnp.float32) + b.astype(jnp.float32)).astype(jnp.bfloat16)
        a = lax.ppermute(send_a, axis, [(i, i + 1) for i in range(step)])
        b = lax.ppermute(send_b, axis, [(count - 1 - i, count - 2 - i) for i in range(step)])
        a, b = lax.optimization_barrier((a, b))
    return (
        block(index).astype(jnp.float32) + a.astype(jnp.float32) + b.astype(jnp.float32)
    )


def total_over(value, axis):
    count = lax.axis_size(axis)
    total = value
    for by in range(1, count):
        pairs = [(i, (i + by) % count) for i in range(count)]
        total = total + lax.ppermute(value, axis, pairs)
    return total


def swap(by):
    return [(i, i ^ by) for i in range(lax.axis_size("seq"))]


ACROSS = [(0, 1), (1, 0)]


def half_pieces(mine, other):
    half = mine.shape[0] // 2
    start = lax.axis_index("grp") * half
    near = lax.ppermute(lax.dynamic_slice_in_dim(mine, start, half), "seq", swap(2))
    far = lax.ppermute(lax.dynamic_slice_in_dim(other, start, half), "seq", swap(3))
    core = lax.ppermute(other, "seq", swap(1))
    near_x = lax.ppermute(near, "grp", ACROSS)
    far_x = lax.ppermute(far, "grp", ACROSS)
    return mine, core, [near, near_x], [far, far_x]


def full_pieces(weight, chunks):
    half = weight.shape[0] // 2
    part = half // chunks
    near, far = [], []
    core = lax.ppermute(weight, "seq", swap(1))
    for i in range(chunks):
        start = lax.axis_index("grp") * half + i * part
        mine = lax.dynamic_slice_in_dim(weight, start, part)
        got = lax.ppermute(mine, "seq", swap(2))
        more = lax.ppermute(got, "grp", ACROSS)
        near += [got, more]
        far += [lax.ppermute(got, "seq", swap(1)), lax.ppermute(more, "seq", swap(1))]
    return weight, core, near, far


def on_device(*args):
    return paired_device(*args)


def paired_device(
    prompt, cont_ids, embed, pre_gain, w_query, w_keyval, q_gain, k_gain, w_out, post_gain
):
    tok_rows, local_cols = prompt.shape
    n_seq = lax.axis_size("seq")
    n_tp = lax.axis_size("tp")
    seq_index = lax.axis_index("seq")
    tp_index = lax.axis_index("tp")
    core_index = seq_index & 1
    full_width = local_cols * n_tp
    cont_count, cont_len = cont_ids.shape
    own_conts = cont_count // n_seq
    cont_rows = own_conts * cont_len
    head_dim = q_gain.shape[0]
    pos = jnp.stack([seq_index, tp_index, lax.axis_index("grp")]).astype(jnp.int32)

    prompt_t = prompt.T
    prompt_x = lax.all_gather(prompt_t, "tp", axis=0)

    def half_of(weight, side):
        size = weight.shape[-1] // 2
        part = lax.dynamic_slice_in_dim(weight, side * size, size, weight.ndim - 1)
        return part.reshape(part.shape[0], -1)

    kv_pieces = half_pieces(half_of(w_keyval, core_index), half_of(w_keyval, 1 - core_index))
    q_pieces = half_pieces(half_of(w_query, core_index), half_of(w_query, 1 - core_index))
    out_pieces = full_pieces(w_out.T, 2)

    ids = cont_ids.reshape(n_seq, cont_rows)
    held = []
    for parts in ((1, 3), (0, 2)):
        wanted = [lax.dynamic_index_in_dim(ids, seq_index ^ r, 0, False) for r in parts]
        start = seq_index * embed.shape[0]
        held.append(pick_rows(embed.T, jnp.concatenate(wanted), start))
    give, keep = held
    keep = keep + lax.ppermute(give, "seq", swap(1))
    theirs = lax.ppermute(keep[:, cont_rows:], "seq", swap(2))
    mine = keep[:, :cont_rows] + theirs
    cont_t = (mine.astype(jnp.float32) * math.sqrt(full_width)).astype(jnp.bfloat16)
    cont_x = lax.all_gather(cont_t, "tp", axis=0)

    def turns(positions):
        lane = jnp.arange(head_dim, dtype=jnp.int32)
        half = head_dim // 2
        freqs = rope_base ** (-((lane % half).astype(jnp.float32) * 2.0) / head_dim)
        angles = positions.astype(jnp.float32)[:, None] * freqs[None, :]
        return jnp.cos(angles), jnp.sin(angles) * jnp.where(lane < half, -1.0, 1.0)

    row = jnp.arange(2 * tok_rows, dtype=jnp.int32)
    block = jnp.where(row < tok_rows, seq_index, seq_index ^ 1)
    prompt_turns = turns(block * tok_rows + row % tok_rows)
    spot = jnp.arange(2 * cont_rows, dtype=jnp.int32) % cont_len
    cont_turns = turns(n_seq * tok_rows + spot)

    gain = pre_gain.reshape(n_tp, local_cols)
    kv_cols = w_keyval.shape[2] // 2
    q_cols = w_query.shape[1] // 2

    def rows_of(x):
        normed = norm_rows(pos, gain, x)
        return [normed, lax.ppermute(normed, "seq", swap(1))]

    def shares(mixed):
        return mixed[0], lax.ppermute(mixed[1], "seq", swap(1))

    rows_p = rows_of(prompt_x)
    here_kv = project(kv_cols, pos, rows_p, k_gain, *prompt_turns, kv_pieces)
    there_kv = lax.ppermute(here_kv, "seq", swap(2))
    queries_p = project(q_cols, pos, rows_p, q_gain, *prompt_turns, q_pieces)
    mixed_p = attend_rows(prompt_kernel, head_dim, pos, queries_p, here_kv, there_kv, None)
    pair_p = shares(mixed_p)
    rows_c = rows_of(cont_x)
    cont_kv = project(kv_cols, pos, rows_c, k_gain, *cont_turns, kv_pieces)
    queries_c = project(q_cols, pos, rows_c, q_gain, *cont_turns, q_pieces)
    kernel = functools.partial(cont_kernel, cont_len, tok_rows)
    mixed_c = attend_rows(kernel, head_dim, pos, queries_c, here_kv, there_kv, cont_kv)
    pair_c = shares(mixed_c)
    part_p = project_out(pos, *pair_p, out_pieces)
    part_c = project_out(pos, *pair_c, out_pieces)
    gain_part = lax.dynamic_slice_in_dim(post_gain, tp_index * local_cols, local_cols)[:, None]

    attn_p = lax.psum_scatter(part_p, "tp", scatter_dimension=0).astype(jnp.float32)
    attn_c = line_scatter(part_c, "tp")
    row_sq = jnp.concatenate(
        [jnp.sum(attn * attn, axis=0, keepdims=True) for attn in (attn_p, attn_c)], axis=1
    )
    factor = lax.rsqrt(total_over(row_sq, "tp") / full_width + eps_norm)

    def finish(attn, factor, rows_t):
        return (rows_t.astype(jnp.float32) + attn * factor * gain_part).astype(jnp.bfloat16)

    prompt_out = finish(attn_p, factor[:, :tok_rows], prompt_t).T
    cont_out = finish(attn_c, factor[:, tok_rows:], cont_t).T
    return (prompt_out, cont_out.reshape(own_conts, cont_len, local_cols))


def solution(mesh):
    shape = mesh.shape
    paired = shape["grp"] == 2 and shape["seq"] == 4 and shape["tp"] == 4
    return jax.shard_map(
        on_device if paired else plain_device,
        mesh=mesh,
        in_specs=(
            P(("grp", "seq"), "tp"),
            P("grp", None),
            P("seq", "tp"),
            P(),
            P("seq", "tp"),
            P("seq", None, "tp"),
            P(),
            P(),
            P("tp", "seq"),
            P(),
        ),
        out_specs=(P(("grp", "seq"), "tp"), P(("grp", "seq"), None, "tp")),
        check_vma=False,
    )
```

```python
import functools
import math

import jax
import jax.numpy as jnp
from jax import lax
from jax.experimental import pallas as pl
from jax.experimental.pallas import tpu as pltpu
from jax.sharding import PartitionSpec as P


WINDOW = 1024


eps_norm = 1e-06
query_scalar = 168.0
rope_base = 10000.0


def from_behind(value, axis, by):
    count = lax.axis_size(axis)
    pairs = [(i, i + by) for i in range(count) if 0 <= i + by < count]
    return lax.ppermute(value, axis, pairs)


def from_root(value, axis, root):
    mine = lax.axis_index(axis) == root
    return lax.psum(jnp.where(mine, value, jnp.zeros_like(value)), axis)


def rms_scale(values, gain):
    mean_sq = jnp.mean(values * values, axis=-1, keepdims=True)
    return values * lax.rsqrt(mean_sq + eps_norm) * gain


def rotate(values, positions):
    half = values.shape[-1] // 2
    freqs = rope_base ** (
        -(jnp.arange(half, dtype=jnp.int32).astype(jnp.float32) * 2.0) / values.shape[-1]
    )
    angles = positions.astype(jnp.float32)[:, None] * freqs[None, :]
    cosine = jnp.cos(angles)[:, None, :]
    sine = jnp.sin(angles)[:, None, :]
    first = values[..., :half]
    second = values[..., half:]
    return jnp.concatenate(
        [first * cosine - second * sine, second * cosine + first * sine], axis=-1
    )


def attend(queries, keys, values, allowed):
    rows, heads, width = queries.shape
    kv_heads = keys.shape[1]
    grouped = queries.reshape(rows, kv_heads, heads // kv_heads, width)
    scores = jnp.einsum(
        "qkgd,nkd->kgqn", grouped, keys, preferred_element_type=jnp.float32
    ) * query_scalar ** (-0.5)
    scores = jnp.where(allowed[None, None], scores, -1e30)
    top = jnp.max(scores, axis=-1, keepdims=True)
    weights = jnp.exp(scores - top)
    weights = (weights / jnp.sum(weights, axis=-1, keepdims=True)).astype(jnp.bfloat16)
    mixed = jnp.einsum("kgqn,nkd->qkgd", weights, values, preferred_element_type=jnp.float32)
    return mixed.reshape(rows, heads * width).astype(jnp.bfloat16)


def plain_device(
    prompt, cont_ids, embed, pre_gain, w_query, w_keyval, q_gain, k_gain, w_out, post_gain
):
    tok_rows, local_cols = prompt.shape
    n_seq = lax.axis_size("seq")
    n_tp = lax.axis_size("tp")
    seq_index = lax.axis_index("seq")
    tp_index = lax.axis_index("tp")
    full_width = local_cols * n_tp
    cont_count, cont_len = cont_ids.shape
    own_conts = cont_count // n_seq
    cont_rows = own_conts * cont_len
    vocab_rows = embed.shape[0]
    flat_ids = cont_ids.reshape(-1)
    vocab_start = seq_index * vocab_rows
    chosen = flat_ids - vocab_start
    inside = (chosen >= 0) & (chosen < vocab_rows)
    picked = jnp.take(embed, jnp.clip(chosen, 0, vocab_rows - 1), axis=0)
    embedded = lax.psum_scatter(
        jnp.where(inside[:, None], picked.astype(jnp.float32), 0.0).astype(jnp.bfloat16),
        "seq",
        scatter_dimension=0,
        tiled=True,
    ).astype(jnp.float32)
    cont_x = (embedded * math.sqrt(full_width)).astype(jnp.bfloat16)
    rows_x = jnp.concatenate([prompt, cont_x], axis=0)
    whole = lax.all_gather(rows_x, "tp", axis=1, tiled=True)
    normed = rms_scale(whole.astype(jnp.float32), pre_gain).astype(jnp.bfloat16)
    all_rows = normed.shape[0]
    q_cols = w_query.shape[1]
    kv_cols = w_keyval.shape[2]
    query_part = jnp.dot(
        normed,
        lax.all_gather(w_query, "seq", axis=0, tiled=True),
        preferred_element_type=jnp.float32,
    )
    kv_part = jnp.einsum(
        "rd,dcf->rcf",
        normed,
        lax.all_gather(w_keyval, "seq", axis=0, tiled=True),
        preferred_element_type=jnp.float32,
    )
    head_dim = q_gain.shape[0]
    q_heads = q_cols // head_dim
    kv_heads = kv_cols // head_dim
    tokens_total = n_seq * tok_rows
    positions = jnp.concatenate(
        [
            seq_index * tok_rows + jnp.arange(tok_rows, dtype=jnp.int32),
            tokens_total + jnp.arange(cont_rows, dtype=jnp.int32) % cont_len,
        ]
    )
    queries = rotate(
        rms_scale(query_part.reshape(all_rows, q_heads, head_dim), q_gain), positions
    ).astype(jnp.bfloat16)
    keys = rotate(
        rms_scale(kv_part[:, 0].reshape(all_rows, kv_heads, head_dim), k_gain), positions
    ).astype(jnp.bfloat16)
    values = kv_part[:, 1].astype(jnp.bfloat16)
    keyval = jnp.stack([keys.reshape(all_rows, kv_cols), values], axis=1)
    prompt_kv = keyval[:tok_rows]
    cont_kv = keyval[tok_rows:]
    reach = WINDOW // tok_rows
    earlier = []
    moving = prompt_kv
    for _ in range(reach):
        moving = from_behind(moving, "seq", 1)
        earlier = [moving] + earlier
    band = jnp.concatenate(earlier + [prompt_kv], axis=0)
    q_pos = positions[:tok_rows]
    key_pos = seq_index * tok_rows - reach * tok_rows + jnp.arange(band.shape[0], dtype=jnp.int32)
    allowed = (
        (key_pos[None, :] <= q_pos[:, None])
        & (key_pos[None, :] > q_pos[:, None] - WINDOW)
        & (key_pos[None, :] >= 0)
    )
    prompt_mix = attend(
        queries[:tok_rows],
        band[:, 0].reshape(-1, kv_heads, head_dim),
        band[:, 1].reshape(-1, kv_heads, head_dim),
        allowed,
    )
    final = from_root(band[band.shape[0] - WINDOW :], "seq", n_seq - 1)
    spots = jnp.arange(cont_len, dtype=jnp.int32)
    allowed_cont = jnp.concatenate(
        [
            jnp.arange(WINDOW, dtype=jnp.int32)[None, :] > spots[:, None],
            spots[None, :] <= spots[:, None],
        ],
        axis=1,
    )
    cont_q = queries[tok_rows:].reshape(own_conts, cont_len, q_heads, head_dim)
    cont_keys = cont_kv.reshape(own_conts, cont_len, 2, kv_cols)

    def one_cont(query_block, key_block):
        joined = jnp.concatenate([final, key_block], axis=0)
        return attend(
            query_block,
            joined[:, 0].reshape(-1, kv_heads, head_dim),
            joined[:, 1].reshape(-1, kv_heads, head_dim),
            allowed_cont,
        )

    cont_mix = jax.vmap(one_cont)(cont_q, cont_keys).reshape(cont_rows, q_cols)
    mixed = jnp.concatenate([prompt_mix, cont_mix], axis=0)
    partial_rows = jnp.dot(
        mixed, lax.all_gather(w_out, "seq", axis=1, tiled=True), preferred_element_type=jnp.float32
    )
    attn_proj = lax.psum_scatter(
        partial_rows.astype(jnp.bfloat16), "tp", scatter_dimension=1, tiled=True
    ).astype(jnp.float32)
    row_sq = lax.psum(jnp.sum(attn_proj * attn_proj, axis=1), "tp")
    factor = lax.rsqrt(row_sq / full_width + eps_norm)
    gain_part = lax.dynamic_slice_in_dim(post_gain, tp_index * local_cols, local_cols)
    result = (rows_x.astype(jnp.float32) + attn_proj * factor[:, None] * gain_part).astype(
        jnp.bfloat16
    )
    return (result[:tok_rows], result[tok_rows:].reshape(own_conts, cont_len, local_cols))


ANY = pl.BlockSpec(memory_space=pl.ANY)
SMEM = pl.BlockSpec(memory_space=pltpu.SMEM)
VMEM = pl.BlockSpec(memory_space=pltpu.VMEM)
BATCH = 8


def pick_kernel(info, emb, lanes, listed, ids, out, buf, held, acc, sems):
    rounds = (info[0] + BATCH - 1) // BATCH
    width = BATCH * 128
    per_group = 128 // BATCH

    def copies(step, slot):
        for b in range(BATCH):
            block = info[1 + step * BATCH + b]
            yield pltpu.make_async_copy(
                emb.at[:, pl.ds(pl.multiple_of(block * 128, 128), 128)],
                buf.at[slot, :, pl.ds(b * 128, 128)],
                sems.at[slot, b],
            )

    acc[...] = jnp.zeros_like(acc)
    held[...] = jnp.zeros_like(held)

    @pl.when(rounds > 0)
    def _():
        for copy in copies(0, 0):
            copy.start()

    def body(step, carry):
        slot = lax.rem(step, 2)
        group = step // per_group
        within = step - group * per_group

        @pl.when(step + 1 < rounds)
        def _():
            for copy in copies(step + 1, 1 - slot):
                copy.start()

        for copy in copies(step, slot):
            copy.wait()
        lane = lanes[pl.ds(group, 1), :]
        at = lax.broadcasted_iota(jnp.int32, lane.shape, 1) - within * BATCH
        rel = jnp.where((lane >= 0) & (at >= 0) & (at < BATCH), at * 128 + lane, -1)
        hot = lax.broadcasted_iota(jnp.int32, (width, 128), 0) == rel
        hot = hot.astype(jnp.bfloat16)
        size = held.shape[0] // 4
        keep = jnp.where(within == 0, 0.0, 1.0)
        for start in range(0, held.shape[0], size):
            span = pl.ds(start, size)
            got = jnp.dot(buf[slot, span, :], hot, preferred_element_type=jnp.float32)
            held[span, :] = held[span, :] * keep + got

        @pl.when((within == per_group - 1) | (step == rounds - 1))
        def _():
            name = listed[pl.ds(pl.multiple_of(group * 128, 128), 128), :]
            spread = (name == ids[...]).astype(jnp.bfloat16)
            acc[...] += jnp.dot(
                held[...].astype(jnp.bfloat16), spread, preferred_element_type=jnp.float32
            )

        return carry

    lax.fori_loop(0, rounds, body, 0)
    out[...] = acc[...].astype(jnp.bfloat16)


def pick_rows(emb_t, flat_ids, vocab_start):
    width, vocab = emb_t.shape
    rows = flat_ids.shape[0]
    ids = flat_ids - vocab_start
    ids = jnp.where((ids >= 0) & (ids < vocab), ids, -2)
    number = jnp.arange(rows, dtype=jnp.int32)
    same = (ids[:, None] == ids[None, :]) & (number[:, None] < number[None, :])
    first = (ids >= 0) & ~jnp.any(same, axis=0)
    rank = jnp.sum(
        jnp.where((number[:, None] < number[None, :]) & first[:, None], 1, 0), axis=0
    )
    listed = jnp.max(
        jnp.where(first[None, :] & (rank[None, :] == number[:, None]), ids[None, :], -1),
        axis=1,
    )
    count = jnp.sum(first.astype(jnp.int32))
    info = jnp.concatenate(
        [count[None], jnp.maximum(listed, 0) >> 7, jnp.zeros((BATCH,), jnp.int32)]
    )
    lanes = jnp.where(listed >= 0, listed & 127, -1).reshape(rows // 128, 128)
    return pl.pallas_call(
        pick_kernel,
        out_shape=jax.ShapeDtypeStruct((width, rows), jnp.bfloat16),
        in_specs=[SMEM, ANY, VMEM, VMEM, VMEM],
        out_specs=VMEM,
        scratch_shapes=[
            pltpu.VMEM((2, width, BATCH * 128), jnp.bfloat16),
            pltpu.VMEM((width, 128), jnp.float32),
            pltpu.VMEM((width, rows), jnp.float32),
            pltpu.SemaphoreType.DMA((2, BATCH)),
        ],
        name="pick_rows",
    )(info, emb_t, lanes, listed[:, None], ids[None, :])


def padded(width):
    return -(-width // 128) * 128


def norm_kernel(pos, gain, x, out):
    n, width, rows = x.shape
    pitch = padded(width)
    step = 128
    pieces = [(at, min(step, width - at)) for at in range(0, width, step)]

    def squares(r, total):
        for at, size in pieces:
            block = x[r, at : at + size, :].astype(jnp.float32)
            total = total + jnp.sum((block * block).reshape(size // 8, 8, rows), axis=0)
        return total

    total = lax.fori_loop(0, n, squares, jnp.zeros((8, rows), jnp.float32))
    mean_sq = jnp.sum(total, axis=0, keepdims=True) / (n * width)
    scale = lax.rsqrt(mean_sq + eps_norm)
    for r in range(n):
        for at, size in pieces:
            block = x[r, at : at + size, :].astype(jnp.float32) * scale
            block = block.T * gain[r : r + 1, at : at + size]
            out[:, r * pitch + at : r * pitch + at + size] = block.astype(jnp.bfloat16)


def norm_rows(pos, gain, x):
    n, width, rows = x.shape
    return pl.pallas_call(
        norm_kernel,
        out_shape=jax.ShapeDtypeStruct((rows, n * padded(width)), jnp.bfloat16),
        in_specs=[SMEM, VMEM, VMEM],
        out_specs=VMEM,
        name="norm_rows",
    )(pos, gain, x)


def piece_copies(grp, pieces, store, sems):
    own, core, near, far = pieces
    rows = own.shape[0]
    part = rows // len(near)
    groups = [
        [pltpu.make_async_copy(own, store.at[0], sems.at[0])],
        [pltpu.make_async_copy(core, store.at[1], sems.at[1])],
    ]
    at = 2
    for r, blocks in ((2, near), (3, far)):
        group = []
        for i, block in enumerate(blocks):
            half = grp if i % 2 == 0 else 1 - grp
            start = pl.multiple_of(half * (rows // 2) + (i // 2) * part, 16)
            group.append(
                pltpu.make_async_copy(block, store.at[r, pl.ds(start, part), :], sems.at[at])
            )
            at += 1
        groups.append(group)
    return groups


def proj_kernel(normed_cols, count, parts, pos, gain, cosine, sine, *refs):
    sources, refs = refs[:count], refs[count:]
    near, far = refs[2 : 2 + parts], refs[2 + parts : 2 + 2 * parts]
    out, x, store, total, x_sems, w_sems = refs[2 + 2 * parts :]
    groups = piece_copies(pos[2], (refs[0], refs[1], near, far), store, w_sems)
    width, pitch = store.shape[1], x.shape[2]
    loads = []
    for r in range(4):
        at = 0
        slot = pl.multiple_of(lax.bitwise_xor(pos[0], r) * pitch, 128)
        for i, source in enumerate(sources):
            rows = source.shape[0]
            loads.append(
                pltpu.make_async_copy(
                    source.at[:, pl.ds(slot, pitch)], x.at[r, pl.ds(at, rows), :], x_sems.at[r, i]
                )
            )
            loads[-1].start()
            at += rows
        for copy in groups[r]:
            copy.start()
    head = gain.shape[1]
    for r in range(4):
        for copy in loads[r * count : (r + 1) * count] + groups[r]:
            copy.wait()
        part = jnp.dot(x[r, :, :width], store[r], preferred_element_type=jnp.float32)
        if r == 0:
            total[...] = part
        else:
            total[...] += part
    for start in range(0, out.shape[1], head):
        value = total[:, start : start + head]
        if start < normed_cols:
            mean_sq = jnp.mean(value * value, axis=-1, keepdims=True)
            value = value * lax.rsqrt(mean_sq + eps_norm) * gain[...]
            turned = pltpu.roll(value, head // 2, 1)
            value = value * cosine[...] + turned * sine[...]
        out[:, start : start + head] = value.astype(jnp.bfloat16)


def project(normed_cols, pos, sources, gain, cosine, sine, pieces):
    own, core, near, far = pieces
    width, columns = own.shape
    rows = sum(source.shape[0] for source in sources)
    return pl.pallas_call(
        functools.partial(proj_kernel, normed_cols, len(sources), len(near)),
        out_shape=jax.ShapeDtypeStruct((rows, columns), jnp.bfloat16),
        in_specs=[SMEM] + [VMEM] * 3 + [ANY] * (len(sources) + 2 + 2 * len(near)),
        out_specs=VMEM,
        scratch_shapes=[
            pltpu.VMEM((4, rows, padded(width)), jnp.bfloat16),
            pltpu.VMEM((4, width, columns), jnp.bfloat16),
            pltpu.VMEM((rows, columns), jnp.float32),
            pltpu.SemaphoreType.DMA((4, len(sources))),
            pltpu.SemaphoreType.DMA((2 + 2 * len(near),)),
        ],
        name="project",
    )(pos, gain[None, :], cosine, sine, *sources, own, core, *near, *far)


def softmax_mix(scores, scale, values):
    top = jnp.max(scores, axis=-1, keepdims=True)
    weights = jnp.exp((scores - top) * scale)
    total = jnp.sum(weights, axis=-1, keepdims=True)
    weights = (weights / total).astype(jnp.bfloat16)
    return jnp.dot(weights, values, preferred_element_type=jnp.float32)


def stacked(source, head):
    count = source.shape[1] // head
    return jnp.concatenate([source[:, g * head : (g + 1) * head] for g in range(count)], axis=0)


def unstack(mixed, out, head):
    rows = out.shape[1]
    for g in range(out.shape[2] // head):
        out[0, :, g * head : (g + 1) * head] = mixed[g * rows : (g + 1) * rows].astype(
            jnp.bfloat16
        )


CONTRACT = (((1,), (1,)), ((), ()))


def prompt_kernel(pos, q, k0, k2, v0, v2, out):
    own_index = pos[0]
    block = lax.bitwise_xor(own_index, pl.program_id(1))
    tokens, head = q.shape[0], k0.shape[1]
    keys = [k0[:tokens], k0[tokens:], k2[:tokens], k2[tokens:]]
    q_own = stacked(q, head)
    rows = q_own.shape[0]
    q_at = lax.rem(lax.broadcasted_iota(jnp.int32, (rows, tokens), 0), tokens)
    ahead = q_at - lax.broadcasted_iota(jnp.int32, (rows, tokens), 1)
    blocks = []
    for r in range(4):
        gap = ahead + (block - lax.bitwise_xor(own_index, r)) * tokens
        score = lax.dot_general(q_own, keys[r], CONTRACT, preferred_element_type=jnp.float32)
        blocks.append(jnp.where((gap >= 0) & (gap < WINDOW), score, -1e30))
    values = jnp.concatenate([v0[...], v2[...]], axis=0)
    scale = query_scalar ** (-0.5)
    unstack(softmax_mix(jnp.concatenate(blocks, axis=1), scale, values), out, head)


def cont_kernel(cont_len, tokens, pos, q, k0, k2, v0, v2, ck, cv, out):
    own_index = pos[0]
    conts, head = q.shape[0], k0.shape[1]
    keys = [k0[:tokens], k0[tokens:], k2[:tokens], k2[tokens:]]
    q_cont = stacked(q, head)
    rows = q_cont.shape[0]
    q_row = lax.rem(lax.broadcasted_iota(jnp.int32, (rows, tokens), 0), conts)
    late = lax.broadcasted_iota(jnp.int32, (rows, tokens), 1) - lax.rem(q_row, cont_len)
    blocks = []
    for r in range(4):
        base = lax.bitwise_xor(own_index, r) * tokens - (4 * tokens - WINDOW)
        score = lax.dot_general(q_cont, keys[r], CONTRACT, preferred_element_type=jnp.float32)
        blocks.append(jnp.where(late + base > 0, score, -1e30))
    q_row = lax.rem(lax.broadcasted_iota(jnp.int32, (rows, conts), 0), conts)
    k_row = lax.broadcasted_iota(jnp.int32, (rows, conts), 1)
    same = (q_row // cont_len) == (k_row // cont_len)
    score = lax.dot_general(q_cont, ck[...], CONTRACT, preferred_element_type=jnp.float32)
    blocks.append(jnp.where(same & (k_row <= q_row), score, -1e30))
    values = jnp.concatenate([v0[...], v2[...], cv[...]], axis=0)
    scale = query_scalar ** (-0.5)
    unstack(softmax_mix(jnp.concatenate(blocks, axis=1), scale, values), out, head)


def attend_rows(kernel, head, pos, queries, here_kv, there_kv, cont_kv):
    rows, q_cols = queries.shape[0] // 2, queries.shape[1]
    span = here_kv.shape[0]
    kv_heads = here_kv.shape[1] // (2 * head)
    wide = q_cols // kv_heads

    def column(shift):
        return pl.BlockSpec((span, head), lambda h, b, pos: (0, h + shift))

    def cont_column(shift):
        return pl.BlockSpec((rows, head), lambda h, b, pos: (b, h + shift))

    specs = [pl.BlockSpec((rows, wide), lambda h, b, pos: (b, h))]
    specs += [column(0), column(0), column(kv_heads), column(kv_heads)]
    operands = [queries, here_kv, there_kv, here_kv, there_kv]
    if cont_kv is not None:
        specs += [cont_column(0), cont_column(kv_heads)]
        operands += [cont_kv, cont_kv]
    return pl.pallas_call(
        kernel,
        out_shape=jax.ShapeDtypeStruct((2, rows, q_cols), jnp.bfloat16),
        grid_spec=pltpu.PrefetchScalarGridSpec(
            num_scalar_prefetch=1,
            grid=(kv_heads, 2),
            in_specs=specs,
            out_specs=pl.BlockSpec((1, rows, wide), lambda h, b, pos: (b, 0, h)),
        ),
        name="attend_rows",
    )(pos, *operands)


def out_kernel(parts, pos, mine, theirs, *refs):
    seq_index, grp = pos[0], pos[2]
    core = lax.bitwise_and(seq_index, 1)
    near, far = refs[2 : 2 + parts], refs[2 + parts : 2 + 2 * parts]
    out, mixed, turned, store, m_sems, sems = refs[2 + 2 * parts :]
    groups = piece_copies(grp, (refs[0], refs[1], near, far), store, sems)
    half = mine.shape[1]
    loads = []
    for i, (source, side) in enumerate(((mine, core), (theirs, 1 - core))):
        columns = pl.ds(pl.multiple_of(side * half, 128), half)
        loads.append(pltpu.make_async_copy(source, mixed.at[:, columns], m_sems.at[i]))
        loads[i].start()
    for group in groups:
        for copy in group:
            copy.start()
    for copy in loads:
        copy.wait()
    turned[...] = mixed[...].T
    for r in range(4):
        for copy in groups[r]:
            copy.wait()
        slot = lax.bitwise_xor(seq_index, r)
        size = store.shape[1] // 4
        for at in range(0, store.shape[1], size):
            out[slot, at : at + size] = jnp.dot(
                store[r, at : at + size], turned[...], preferred_element_type=jnp.float32
            ).astype(jnp.bfloat16)


def project_out(pos, mine, theirs, pieces):
    own, core, near, far = pieces
    width, size = own.shape
    rows = mine.shape[0]
    return pl.pallas_call(
        functools.partial(out_kernel, len(near)),
        out_shape=jax.ShapeDtypeStruct((4, width, rows), jnp.bfloat16),
        in_specs=[SMEM] + [ANY] * (4 + 2 * len(near)),
        out_specs=VMEM,
        scratch_shapes=[
            pltpu.VMEM((rows, size), jnp.bfloat16),
            pltpu.VMEM((size, rows), jnp.bfloat16),
            pltpu.VMEM((4, width, size), jnp.bfloat16),
            pltpu.SemaphoreType.DMA((2,)),
            pltpu.SemaphoreType.DMA((2 + 2 * len(near),)),
        ],
        name="project_out",
    )(pos, mine, theirs, own, core, *near, *far)


def direct_scatter(parts, axis):
    count = lax.axis_size(axis)
    index = lax.axis_index(axis)

    def block(at):
        return lax.dynamic_index_in_dim(parts, at % count, 0, False)

    got = [
        lax.ppermute(block(index + by), axis, [(i, (i + by) % count) for i in range(count)])
        for by in range(1, count)
    ]
    return sum((part.astype(jnp.float32) for part in got), block(index).astype(jnp.float32))


def total_over(value, axis):
    count = lax.axis_size(axis)
    total = value
    for by in range(1, count):
        pairs = [(i, (i + by) % count) for i in range(count)]
        total = total + lax.ppermute(value, axis, pairs)
    return total


def swap(by):
    return [(i, i ^ by) for i in range(lax.axis_size("seq"))]


ACROSS = [(0, 1), (1, 0)]


def half_pieces(mine, other):
    half = mine.shape[0] // 2
    start = lax.axis_index("grp") * half
    near = lax.ppermute(lax.dynamic_slice_in_dim(mine, start, half), "seq", swap(2))
    far = lax.ppermute(lax.dynamic_slice_in_dim(other, start, half), "seq", swap(3))
    core = lax.ppermute(other, "seq", swap(1))
    near_x = lax.ppermute(near, "grp", ACROSS)
    far_x = lax.ppermute(far, "grp", ACROSS)
    return mine, core, [near, near_x], [far, far_x]


def full_pieces(weight, chunks):
    half = weight.shape[0] // 2
    part = half // chunks
    near, far = [], []
    core = lax.ppermute(weight, "seq", swap(1))
    for i in range(chunks):
        start = lax.axis_index("grp") * half + i * part
        mine = lax.dynamic_slice_in_dim(weight, start, part)
        got = lax.ppermute(mine, "seq", swap(2))
        more = lax.ppermute(got, "grp", ACROSS)
        near += [got, more]
        far += [lax.ppermute(got, "seq", swap(1)), lax.ppermute(more, "seq", swap(1))]
    return weight, core, near, far


def on_device(*args):
    return paired_device(*args)


def paired_device(
    prompt, cont_ids, embed, pre_gain, w_query, w_keyval, q_gain, k_gain, w_out, post_gain
):
    tok_rows, local_cols = prompt.shape
    n_seq = lax.axis_size("seq")
    n_tp = lax.axis_size("tp")
    seq_index = lax.axis_index("seq")
    tp_index = lax.axis_index("tp")
    core_index = seq_index & 1
    full_width = local_cols * n_tp
    cont_count, cont_len = cont_ids.shape
    own_conts = cont_count // n_seq
    cont_rows = own_conts * cont_len
    head_dim = q_gain.shape[0]
    pos = jnp.stack([seq_index, tp_index, lax.axis_index("grp")]).astype(jnp.int32)

    prompt_t = prompt.T
    prompt_x = lax.all_gather(prompt_t, "tp", axis=0)

    def half_of(weight, side):
        size = weight.shape[-1] // 2
        part = lax.dynamic_slice_in_dim(weight, side * size, size, weight.ndim - 1)
        return part.reshape(part.shape[0], -1)

    kv_pieces = half_pieces(half_of(w_keyval, core_index), half_of(w_keyval, 1 - core_index))
    q_pieces = half_pieces(half_of(w_query, core_index), half_of(w_query, 1 - core_index))
    out_pieces = full_pieces(w_out.T, 2)

    ids = cont_ids.reshape(n_seq, cont_rows)
    held = []
    for parts in ((1, 3), (0, 2)):
        wanted = [lax.dynamic_index_in_dim(ids, seq_index ^ r, 0, False) for r in parts]
        start = seq_index * embed.shape[0]
        held.append(pick_rows(embed.T, jnp.concatenate(wanted), start))
    give, keep = held
    keep = keep + lax.ppermute(give, "seq", swap(1))
    theirs = lax.ppermute(keep[:, cont_rows:], "seq", swap(2))
    mine = keep[:, :cont_rows] + theirs
    cont_t = (mine.astype(jnp.float32) * math.sqrt(full_width)).astype(jnp.bfloat16)
    cont_x = lax.all_gather(cont_t, "tp", axis=0)

    def turns(positions):
        lane = jnp.arange(head_dim, dtype=jnp.int32)
        half = head_dim // 2
        freqs = rope_base ** (-((lane % half).astype(jnp.float32) * 2.0) / head_dim)
        angles = positions.astype(jnp.float32)[:, None] * freqs[None, :]
        return jnp.cos(angles), jnp.sin(angles) * jnp.where(lane < half, -1.0, 1.0)

    row = jnp.arange(2 * tok_rows, dtype=jnp.int32)
    block = jnp.where(row < tok_rows, seq_index, seq_index ^ 1)
    prompt_turns = turns(block * tok_rows + row % tok_rows)
    spot = jnp.arange(2 * cont_rows, dtype=jnp.int32) % cont_len
    cont_turns = turns(n_seq * tok_rows + spot)

    gain = pre_gain.reshape(n_tp, local_cols)
    kv_cols = w_keyval.shape[2] // 2
    q_cols = w_query.shape[1] // 2

    def rows_of(x):
        normed = norm_rows(pos, gain, x)
        return [normed, lax.ppermute(normed, "seq", swap(1))]

    def shares(mixed):
        return mixed[0], lax.ppermute(mixed[1], "seq", swap(1))

    rows_p = rows_of(prompt_x)
    here_kv = project(kv_cols, pos, rows_p, k_gain, *prompt_turns, kv_pieces)
    there_kv = lax.ppermute(here_kv, "seq", swap(2))
    queries_p = project(q_cols, pos, rows_p, q_gain, *prompt_turns, q_pieces)
    mixed_p = attend_rows(prompt_kernel, head_dim, pos, queries_p, here_kv, there_kv, None)
    pair_p = shares(mixed_p)
    rows_c = rows_of(cont_x)
    cont_kv = project(kv_cols, pos, rows_c, k_gain, *cont_turns, kv_pieces)
    queries_c = project(q_cols, pos, rows_c, q_gain, *cont_turns, q_pieces)
    kernel = functools.partial(cont_kernel, cont_len, tok_rows)
    mixed_c = attend_rows(kernel, head_dim, pos, queries_c, here_kv, there_kv, cont_kv)
    pair_c = shares(mixed_c)
    part_p = project_out(pos, *pair_p, out_pieces)
    part_c = project_out(pos, *pair_c, out_pieces)
    gain_part = lax.dynamic_slice_in_dim(post_gain, tp_index * local_cols, local_cols)[:, None]

    attn_p = lax.psum_scatter(part_p, "tp", scatter_dimension=0).astype(jnp.float32)
    attn_c = direct_scatter(part_c, "tp")
    sum_p = jnp.sum(attn_p * attn_p, axis=0, keepdims=True)
    sum_c = jnp.sum(attn_c * attn_c, axis=0, keepdims=True)
    row_sq = jnp.concatenate([sum_p, sum_c], axis=1)
    factor = lax.rsqrt(total_over(row_sq, "tp") / full_width + eps_norm)

    def finish(attn, factor, rows_t):
        return (rows_t.astype(jnp.float32) + attn * factor * gain_part).astype(jnp.bfloat16)

    prompt_out = finish(attn_p, factor[:, :tok_rows], prompt_t).T
    cont_out = finish(attn_c, factor[:, tok_rows:], cont_t).T
    return (prompt_out, cont_out.reshape(own_conts, cont_len, local_cols))


def solution(mesh):
    shape = mesh.shape
    paired = shape["grp"] == 2 and shape["seq"] == 4 and shape["tp"] == 4
    return jax.shard_map(
        on_device if paired else plain_device,
        mesh=mesh,
        in_specs=(
            P(("grp", "seq"), "tp"),
            P("grp", None),
            P("seq", "tp"),
            P(),
            P("seq", "tp"),
            P("seq", None, "tp"),
            P(),
            P(),
            P("tp", "seq"),
            P(),
        ),
        out_specs=(P(("grp", "seq"), "tp"), P(("grp", "seq"), None, "tp")),
        check_vma=False,
    )
```
